512 devices in a mesh: lat: 16 (over y, x), lon: 32 (over z, core).
Axes of the slice: x: 4, y: 4, z: 16, core: 2. Of those that a mesh axis runs over, the one named last changes fastest.
Arguments:
- prior_state: bfloat16 [2, 4, 80, 128, 4096], P(None, None, None, 'lat', 'lon'), may hold values from -6 to 6
- courant: float32 [2, 4, 128, 4096], P(None, None, 'lat', 'lon'), may hold values from -0.45 to 0.45
- obs_tile: int32 [64], replicated, may hold values from 0 to 511, as said below
- obs_site: int32 [64], replicated, may hold values from 0 to 8191
- obs_value: float32 [64], replicated, may hold values from -6 to 6
- obs_var: float32 [64], replicated, may hold values from 0.2 to 2
- loc_bits: int32 [64, 18], replicated, may hold values from 0 to 1073741823
- batch_order: int32 [4], replicated, may hold values from 0 to 3, each once
Outputs:
- analysis: bfloat16 [2, 4, 80, 128, 4096], P(None, None, None, 'lat', 'lon')
The draws below stay inside these ranges and needn't reach their ends.
Inputs may be any that keep to these rules, and one draw needn't show every extreme that they name: `obs_tile`: in each batch of 16 consecutive observations one tile owns exactly 4 observations and every other tile at most one. `loc_bits`: bits of tiles numbered 512 or more are not read.
All inputs are finite; a program needn't handle non-finite values.
Results may differ from the reference program's by a relative error of at most 0.0013.
Values may be sent and summed in bfloat16 or wider, within the bound.
A program may use at most 64 MiB of HBM per device.

```python
import math
import jax
import jax.numpy as jnp
from jax import lax

FIELD_COUNT = 2
LEVEL_COUNT = 4
ENSEMBLE_SIZE = 80
TILE_LAT_ROWS = 8
TILE_LON_COLUMNS = 128
OBSERVED_BATCH = 16
BATCHES = 4
CAP = 4
NOBS = 64
WORDS = 18
NLAT = 128
NLON = 4096
N_LAT = 16
N_LON = 32
DEVICES = 512


def draw_obs_tile(key, part):
    collected = []
    for batch_index in range(BATCHES):
        subkey = jax.random.fold_in(key, 7919 + batch_index)
        key_tiles, key_shuffle = jax.random.split(subkey)
        shuffled = jax.random.permutation(key_tiles, DEVICES).astype(jnp.int32)
        crowded = jnp.full((CAP,), shuffled[0], jnp.int32)
        singles = shuffled[1:OBSERVED_BATCH - CAP + 1]
        owner_tiles = jnp.concatenate([crowded, singles])
        placing = jax.random.permutation(key_shuffle, OBSERVED_BATCH)
        collected.append(owner_tiles[placing])
    return jnp.concatenate(collected)


def place_ends(array, key, smallest, largest):
    spot = [jax.random.randint(jax.random.fold_in(key, axis), (), 0, length) for axis, length in enumerate(array.shape)]
    main_axis = array.shape.index(max(array.shape))
    beside = spot[:main_axis] + [(spot[main_axis] + 1) % array.shape[main_axis]] + spot[main_axis + 1:]
    return array.at[tuple(spot)].set(smallest).at[tuple(beside)].set(largest)


def block_scale(own_key, shape, pieces, smallest, largest):
    def one(position, blocks):
        draws = jax.random.uniform(jax.random.fold_in(jax.random.fold_in(own_key, 6), position), (blocks,), jnp.float32, smallest / len(pieces), largest / len(pieces))
        return jnp.repeat(jnp.exp(draws), shape[position] // blocks).reshape((-1,) + (1,) * (len(shape) - position - 1))

    factor_of = one(*pieces[0])
    for cut in pieces[1:]:
        factor_of = factor_of * one(*cut)
    return factor_of


def scatter_about(rng, dims, deviation, bound, cuts=(), held_as=jnp.bfloat16):
    loudness = block_scale(rng, dims, cuts, -0.22, 0.18) if cuts else 1.0
    entries = jax.random.normal(rng, dims, jnp.float32) * deviation * loudness
    return jnp.minimum(jnp.maximum(entries, -bound), bound).astype(held_as)


def setup_inputs(seed: int = 0) -> dict:
    key_list = jax.random.split(jax.random.key(seed), 9)
    prior_state = scatter_about(key_list[0], (FIELD_COUNT, LEVEL_COUNT, ENSEMBLE_SIZE, NLAT, NLON), 1.0, 6.0, ((3, 16), (4, 32)))
    courant = jnp.clip(jax.random.uniform(key_list[1], (2, LEVEL_COUNT, NLAT, NLON), jnp.float32, -0.45, 0.45) * block_scale(key_list[1], (2, LEVEL_COUNT, NLAT, NLON), ((2, 16), (3, 32)), -0.4, 0.0), -0.45, 0.45)
    obs_tile = draw_obs_tile(jax.random.fold_in(key_list[8], 71), 0)
    obs_site = place_ends(jax.random.randint(key_list[3], (NOBS,), 0, FIELD_COUNT * LEVEL_COUNT * TILE_LAT_ROWS * TILE_LON_COLUMNS), jax.random.fold_in(key_list[3], 1), 0, (FIELD_COUNT * LEVEL_COUNT * TILE_LAT_ROWS * TILE_LON_COLUMNS) - 1).astype(jnp.int32)
    obs_value = scatter_about(key_list[4], (NOBS,), 1.5, 6.0, (), jnp.float32)
    obs_var = jnp.clip(jnp.exp(jax.random.uniform(key_list[5], (NOBS,), jnp.float32, math.log(0.2), math.log(2.0))), 0.2, 2.0)
    loc_bits = place_ends(jax.random.randint(key_list[6], (NOBS, WORDS), 0, 1073741824), jax.random.fold_in(key_list[6], 1), 0, 1073741823).astype(jnp.int32)
    batch_order = jax.random.permutation(key_list[7], BATCHES).astype(jnp.int32)
    return {"prior_state": prior_state, "courant": courant, "obs_tile": obs_tile, "obs_site": obs_site, "obs_value": obs_value, "obs_var": obs_var, "loc_bits": loc_bits, "batch_order": batch_order}


EPSILON = 1e-05
HIGHEST_PRECISE = lax.Precision.HIGHEST

def upwind_transport(center_value, west, east, south, north, along_lon, along_lat):
    return center_value - jnp.maximum(along_lon, 0.0) * (center_value - west) - jnp.minimum(along_lon, 0.0) * (east - center_value) - jnp.maximum(along_lat, 0.0) * (center_value - south) - jnp.minimum(along_lat, 0.0) * (north - center_value)

def tile_bits(loc_bits, tile_ids):
    bit_words = jnp.take(loc_bits, tile_ids // 30, axis=1)
    return jnp.bitwise_and(jnp.right_shift(bit_words, (tile_ids % 30)[None, :]), 1).astype(jnp.float32)

def eakf_step(prior_row, obs_val, obs_err, member_list):
    mean_prior = jnp.mean(prior_row)
    anomaly = prior_row - mean_prior
    spread = jnp.sum(anomaly * anomaly) / (member_list - 1) + EPSILON
    post_var = spread * obs_err / (spread + obs_err)
    post_mean = post_var * (mean_prior / spread + obs_val / obs_err)
    factor = jnp.sqrt(obs_err / (spread + obs_err))
    increment = factor * anomaly + post_mean - prior_row
    weights = anomaly / ((member_list - 1) * spread)
    return (increment, weights)

def reference(prior_state, courant, obs_tile, obs_site, obs_value, obs_var, loc_bits, batch_order):
    count_of_cells = TILE_LAT_ROWS * TILE_LON_COLUMNS
    lat_total = TILE_LAT_ROWS * N_LAT
    lon_total = TILE_LON_COLUMNS * N_LON
    field_idx = obs_site // (LEVEL_COUNT * count_of_cells)
    level_position = obs_site // count_of_cells % LEVEL_COUNT
    within = obs_site % count_of_cells
    global_latitude = obs_tile // N_LON * TILE_LAT_ROWS + within // TILE_LON_COLUMNS
    global_longitude = obs_tile % N_LON * TILE_LON_COLUMNS + within % TILE_LON_COLUMNS

    def select_cells(lat_pos, lon_pos):
        inside = ((lat_pos >= 0) & (lat_pos < lat_total)).astype(jnp.float32)
        clipped = jnp.clip(lat_pos, 0, lat_total - 1)
        wrapped = lon_pos % lon_total
        values = prior_state[field_idx, level_position, :, clipped, wrapped].astype(jnp.float32)
        return values * inside[:, None]
    observed_prediction = upwind_transport(select_cells(global_latitude, global_longitude), select_cells(global_latitude, global_longitude - 1), select_cells(global_latitude, global_longitude + 1), select_cells(global_latitude - 1, global_longitude), select_cells(global_latitude + 1, global_longitude), courant[0, level_position, global_latitude, global_longitude][:, None], courant[1, level_position, global_latitude, global_longitude][:, None])
    mask_all = tile_bits(loc_bits, jnp.arange(DEVICES, dtype=jnp.int32))
    transform_list = jnp.broadcast_to(jnp.eye(ENSEMBLE_SIZE, dtype=jnp.float32), (DEVICES, ENSEMBLE_SIZE, ENSEMBLE_SIZE))
    for order_index in range(BATCHES):
        batch_offset = (batch_order[order_index] * OBSERVED_BATCH).astype(jnp.int32)
        owner_tiles = lax.dynamic_slice_in_dim(obs_tile, batch_offset, OBSERVED_BATCH)
        prediction_batch = lax.dynamic_slice_in_dim(observed_prediction, batch_offset, OBSERVED_BATCH, 0)
        obs_values = lax.dynamic_slice_in_dim(obs_value, batch_offset, OBSERVED_BATCH)
        obs_errors = lax.dynamic_slice_in_dim(obs_var, batch_offset, OBSERVED_BATCH)
        mask_batch = lax.dynamic_slice_in_dim(mask_all, batch_offset, OBSERVED_BATCH, 0)
        cross_mask = jnp.take(mask_batch, owner_tiles, axis=1)
        prior_values = jnp.einsum('yz,yzm->ym', prediction_batch, transform_list[owner_tiles], precision=HIGHEST_PRECISE)

        def advance(loop_state, inputs):
            prior_values, transform_list = loop_state
            obs_index, obs_val, obs_err, cross_row, mask_row = inputs
            increment, weights = eakf_step(prior_values[obs_index], obs_val, obs_err, ENSEMBLE_SIZE)
            projected = jnp.dot(prior_values, weights, precision=HIGHEST_PRECISE)
            prior_values = prior_values + cross_row[:, None] * projected[:, None] * increment[None, :]
            turned = jnp.einsum('tef,f->te', transform_list, weights, precision=HIGHEST_PRECISE)
            transform_list = transform_list + mask_row[:, None, None] * turned[:, :, None] * increment[None, None, :]
            return ((prior_values, transform_list), None)
        (prior_values, transform_list), _ = lax.scan(advance, (prior_values, transform_list), (jnp.arange(OBSERVED_BATCH, dtype=jnp.int32), obs_values, obs_errors, cross_mask, mask_batch))
    padded = jnp.pad(prior_state, ((0, 0), (0, 0), (0, 0), (1, 1), (0, 0)))

    def one_row(row_index):
        row_block = lax.dynamic_slice_in_dim(padded, row_index * TILE_LAT_ROWS, TILE_LAT_ROWS + 2, 3).astype(jnp.float32)
        center_value = row_block[:, :, :, 1:-1]
        southern_neighbors = row_block[:, :, :, :-2]
        northern_neighbors = row_block[:, :, :, 2:]
        western_neighbors = jnp.roll(center_value, 1, axis=4)
        eastern_neighbors = jnp.roll(center_value, -1, axis=4)
        wind_per_row = lax.dynamic_slice_in_dim(courant, row_index * TILE_LAT_ROWS, TILE_LAT_ROWS, 2)
        prediction = upwind_transport(center_value, western_neighbors, eastern_neighbors, southern_neighbors, northern_neighbors, wind_per_row[0][None, :, None], wind_per_row[1][None, :, None])
        rows_per_tile = prediction.reshape(FIELD_COUNT, LEVEL_COUNT, ENSEMBLE_SIZE, TILE_LAT_ROWS, N_LON, TILE_LON_COLUMNS)
        row_transforms = lax.dynamic_slice_in_dim(transform_list, row_index * N_LON, N_LON, 0)
        result = jnp.einsum('flesnc,neg->flgsnc', rows_per_tile, row_transforms, precision=HIGHEST_PRECISE)
        return result.reshape(FIELD_COUNT, LEVEL_COUNT, ENSEMBLE_SIZE, TILE_LAT_ROWS, lon_total).astype(jnp.bfloat16)
    row_results = lax.map(one_row, jnp.arange(N_LAT, dtype=jnp.int32))
    return jnp.moveaxis(row_results, 0, 3).reshape(FIELD_COUNT, LEVEL_COUNT, ENSEMBLE_SIZE, lat_total, lon_total)
```

```python
import jax
import jax.numpy as jnp
from jax import lax
from jax.experimental import pallas as pl
from jax.experimental.pallas import tpu as pltpu
from jax.sharding import PartitionSpec as P

MESH = pl.DeviceIdType.MESH
EPSILON = 1e-05
MEMBERS = 80
PLANES = 8
LEVELS = 4
CELLS = 1024
NOBS = 64
BATCH = 16
N_LAT = 16
N_LON = 32
N_Z = 16
GROUP = 32
ROWS = PLANES * MEMBERS
F32 = jnp.float32
BF16 = jnp.bfloat16
VM = pltpu.VMEM
SM = pltpu.SMEM


def spec(space):
    return pl.BlockSpec(memory_space=space)


def edges_kernel(prior_ref, rows_ref, cols_ref, wide):
    lane = lax.broadcasted_iota(jnp.int32, (8, 128), 1)

    def plane(p, _):
        def part(g, acc):
            first, last = acc
            base = p * MEMBERS + g * 16
            for i in range(16):
                x = prior_ref[base + i].astype(F32)
                wide[i * 8 : i * 8 + 8, :] = x
                e = g * 16 + i
                first = jnp.where(lane == e, pltpu.roll(x, e, 1), first)
                last = jnp.where(lane == e, pltpu.roll(x, e + 1, 1), last)
            at = pl.multiple_of(base, 16)
            rows_ref[0, pl.ds(at, 16), :] = wide[pl.ds(7, 16, stride=8), :].astype(BF16)
            rows_ref[1, pl.ds(at, 16), :] = wide[pl.ds(0, 16, stride=8), :].astype(BF16)
            return first, last

        zero = jnp.zeros((8, 128), F32)
        first, last = lax.fori_loop(0, 5, part, (zero, zero))
        cols_ref[0, p] = last.astype(BF16)
        cols_ref[1, p] = first.astype(BF16)
        return 0

    lax.fori_loop(0, PLANES, plane, 0)


def halo_kernel(rows_ref, cols_ref, rows_out, cols_out, send_sem, recv_sem):
    lat = lax.axis_index("lat")
    lon = lax.axis_index("lon")
    north = (lax.rem(lat + 1, N_LAT), lon)
    south = (lax.rem(lat + N_LAT - 1, N_LAT), lon)
    east = (lat, lax.rem(lon + 1, N_LON))
    west = (lat, lax.rem(lon + N_LON - 1, N_LON))
    barrier = pltpu.get_barrier_semaphore()
    for peer in (north, south, east, west):
        pl.semaphore_signal(barrier, inc=1, device_id=peer, device_id_type=MESH)
    pl.semaphore_wait(barrier, 4)
    copies = []
    for n, (src, dst, peer) in enumerate(
        (
            (rows_ref.at[0], rows_out.at[0], north),
            (rows_ref.at[1], rows_out.at[1], south),
            (cols_ref.at[0], cols_out.at[0], east),
            (cols_ref.at[1], cols_out.at[1], west),
        )
    ):
        copy = pltpu.make_async_remote_copy(
            src_ref=src,
            dst_ref=dst,
            send_sem=send_sem.at[n],
            recv_sem=recv_sem.at[n],
            device_id=peer,
            device_id_type=MESH,
        )
        copy.start()
        copies.append(copy)
    for copy in copies:
        copy.wait()


def forecast_kernel(
    me_ref, tile_ref, site_ref, order_ref, prior_ref, wind_ref, rows_ref, cols_ref, f_ref, obs_ref
):
    me = me_ref[0]
    lat = me // N_LON
    lane = lax.broadcasted_iota(jnp.int32, (8, 128), 1)
    sub = lax.broadcasted_iota(jnp.int32, (8, 128), 0)
    has_south = (lat > 0).astype(F32)
    has_north = (lat < N_LAT - 1).astype(F32)

    def plane(p, _):
        level = lax.rem(p, LEVELS)
        cu = wind_ref[level]
        cv = wind_ref[LEVELS + level]
        cu_up, cu_dn = jnp.maximum(cu, 0.0), jnp.minimum(cu, 0.0)
        cv_up, cv_dn = jnp.maximum(cv, 0.0), jnp.minimum(cv, 0.0)
        from_west = cols_ref[0, p].astype(F32)
        from_east = cols_ref[1, p].astype(F32)

        def part(g, _):
            base = p * MEMBERS + g * 16
            at = pl.multiple_of(base, 16)
            south_rows = rows_ref[0, pl.ds(at, 16), :].astype(F32) * has_south
            north_rows = rows_ref[1, pl.ds(at, 16), :].astype(F32) * has_north
            for i in range(16):
                e = g * 16 + i
                x = prior_ref[base + i].astype(F32)
                xw = jnp.where(lane == 0, pltpu.roll(from_west, 128 - e, 1), pltpu.roll(x, 1, 1))
                xe = jnp.where(
                    lane == 127, pltpu.roll(from_east, 127 - e, 1), pltpu.roll(x, 127, 1)
                )
                xs = jnp.where(sub == 0, south_rows[i : i + 1, :], pltpu.roll(x, 1, 0))
                xn = jnp.where(sub == 7, north_rows[i : i + 1, :], pltpu.roll(x, 7, 0))
                f = (
                    x
                    - cu_up * (x - xw)
                    - cu_dn * (xe - x)
                    - cv_up * (x - xs)
                    - cv_dn * (xn - x)
                )
                f_ref[pl.ds(pl.multiple_of((base + i) * 8, 8), 8), :] = f
            return 0

        lax.fori_loop(0, 5, part, 0)
        return 0

    lax.fori_loop(0, PLANES, plane, 0)
    obs_ref[...] = jnp.zeros(obs_ref.shape, F32)

    def one(q, _):
        k = order_ref[q // BATCH] * BATCH + lax.rem(q, BATCH)

        @pl.when(tile_ref[k] == me)
        def _():
            s = site_ref[k]
            p = s // CELLS
            r = lax.rem(s, CELLS) // 128
            c = lax.rem(s, 128)
            cells = f_ref[pl.ds(p * (MEMBERS * 8) + r, MEMBERS, stride=8), :]
            cells = jnp.concatenate([cells, jnp.zeros((128 - MEMBERS, 128), F32)], axis=0)
            pick = (lane == c).astype(F32)
            row = lax.dot_general(
                pick,
                cells,
                (((1,), (1,)), ((), ())),
                precision=lax.Precision.HIGHEST,
                preferred_element_type=F32,
            )
            obs_ref[q // 2, pl.ds(lax.rem(q, 2), 1), :] = row[0:1, :]

        return 0

    lax.fori_loop(0, NOBS, one, 0)


def exchange_kernel(
    obs_ref, out_ref, got1, part, got2, total, got3, send1, recv1, send2, recv2, send3, recv3
):
    lat = lax.axis_index("lat")
    lon = lax.axis_index("lon")
    z = lon // 2
    core = lax.rem(lon, 2)
    mine = lat * 2 + core

    def group_id(n):
        return (n // 2, z * 2 + lax.rem(n, 2))

    def other(d):
        return lax.rem(mine + d, GROUP)

    def other_z(d):
        return lax.rem(z + d, N_Z)

    barrier = pltpu.get_barrier_semaphore()

    def greet(d, _):
        pl.semaphore_signal(barrier, inc=1, device_id=group_id(other(d)), device_id_type=MESH)
        return 0

    def greet_z(d, _):
        pl.semaphore_signal(
            barrier, inc=1, device_id=(lat, other_z(d) * 2 + core), device_id_type=MESH
        )
        return 0

    lax.fori_loop(1, N_Z, greet_z, 0)
    lax.fori_loop(1, GROUP, greet, 0)
    pl.semaphore_wait(barrier, GROUP - 1 + N_Z - 1)

    def copy1(dst, src_slot):
        return pltpu.make_async_remote_copy(
            src_ref=obs_ref.at[dst],
            dst_ref=got1.at[src_slot],
            send_sem=send1.at[dst],
            recv_sem=recv1.at[src_slot],
            device_id=group_id(dst),
            device_id_type=MESH,
        )

    def copy2(dst, src_slot):
        return pltpu.make_async_remote_copy(
            src_ref=part,
            dst_ref=got2.at[src_slot],
            send_sem=send2.at[dst],
            recv_sem=recv2.at[src_slot],
            device_id=(lat, dst * 2 + core),
            device_id_type=MESH,
        )

    def copy3(dst, src_slot):
        return pltpu.make_async_remote_copy(
            src_ref=total,
            dst_ref=got3.at[src_slot],
            send_sem=send3.at[dst],
            recv_sem=recv3.at[src_slot],
            device_id=group_id(dst),
            device_id_type=MESH,
        )

    def loop(first, count, body):
        lax.fori_loop(first, count, lambda d, c: (body(d), c)[1], 0)

    loop(1, GROUP, lambda d: copy1(other(d), mine).start())

    def take1(d, acc):
        src = other(d)
        copy1(src, src).wait_recv()
        return acc + got1[src]

    part[...] = lax.fori_loop(1, GROUP, take1, obs_ref[mine])
    loop(1, N_Z, lambda d: copy2(other_z(d), z).start())

    def take2(d, acc):
        src = other_z(d)
        copy2(src, src).wait_recv()
        return acc + got2[src]

    total[...] = lax.fori_loop(1, N_Z, take2, part[...])
    loop(1, GROUP, lambda d: copy3(other(d), mine).start())
    out_ref[mine] = total[...]

    def take3(d):
        src = other(d)
        copy3(src, src).wait_recv()
        out_ref[src] = got3[src]

    loop(1, GROUP, take3)
    loop(1, GROUP, lambda d: copy1(other(d), mine).wait_send())
    loop(1, N_Z, lambda d: copy2(other_z(d), z).wait_send())
    loop(1, GROUP, lambda d: copy3(other(d), mine).wait_send())


def filter_kernel(
    me_ref,
    tile_ref,
    order_ref,
    value_ref,
    var_ref,
    bits_s_ref,
    bits_ref,
    obs_ref,
    f_ref,
    out_ref,
    table,
    mask_ref,
    turned,
):
    me = me_ref[0]
    for n in range(GROUP):
        table[2 * n : 2 * n + 2, :] = obs_ref[n]
    table[NOBS:, :] = jnp.zeros((128 - NOBS, 128), F32)
    lane = lax.broadcasted_iota(jnp.int32, (1, 128), 1)

    def put(q, row):
        k = order_ref[q // BATCH] * BATCH + lax.rem(q, BATCH)
        return jnp.where(lane == q, tile_ref[k], row)

    owners = lax.fori_loop(0, NOBS, put, jnp.zeros((1, 128), jnp.int32))
    word_of = owners // 30
    bit_of = owners - word_of * 30
    words = bits_ref[...]
    chosen = jnp.zeros((NOBS, 128), jnp.int32)
    for w in range(18):
        chosen = jnp.where(word_of == w, words[:, w : w + 1], chosen)
    mask_ref[...] = jnp.bitwise_and(jnp.right_shift(chosen, bit_of), 1).astype(F32)

    own_word = me // 30
    own_bit = lax.rem(me, 30)
    state = jnp.transpose(table[...])[:MEMBERS, :]
    means = jnp.sum(state, axis=0, keepdims=True) * (1.0 / MEMBERS)
    anomalies = state - means
    eye = (
        lax.broadcasted_iota(jnp.int32, (MEMBERS, 128), 0)
        == lax.broadcasted_iota(jnp.int32, (MEMBERS, 128), 1)
    ).astype(F32)

    def batch(b, carry):
        anomalies, means, turn = carry
        base = order_ref[b] * BATCH
        for j in range(BATCH):
            k = base + j
            r = var_ref[k]
            val = value_ref[k]
            own = jnp.bitwise_and(jnp.right_shift(bits_s_ref[k, own_word], own_bit), 1)
            own = own.astype(F32) * (1.0 / (MEMBERS - 1))
            row = mask_ref[pl.ds(k, 1), :] * (1.0 / (MEMBERS - 1))
            a = jnp.broadcast_to(anomalies[:, j : j + 1], (MEMBERS, 128))
            m = jnp.broadcast_to(means[:, j : j + 1], (1, 128))
            v = jnp.sum(a * a, axis=0, keepdims=True) * (1.0 / (MEMBERS - 1)) + EPSILON
            cov = jnp.sum(anomalies * a, axis=0, keepdims=True) * row
            cov_own = jnp.sum(turn * a, axis=0, keepdims=True) * own
            whole = v + r
            shrink = 1.0 / (whole + jnp.sqrt(r * whole))
            shift = (val - m) / whole
            anomalies = anomalies - (cov * shrink) * a
            means = means + cov * shift
            turn = turn + cov_own * (shift - shrink * a)
        mask_ref[...] = pltpu.roll(mask_ref[...], 128 - BATCH, 1)
        return (
            pltpu.roll(anomalies, 128 - BATCH, 1),
            pltpu.roll(means, 128 - BATCH, 1),
            turn,
        )

    _, _, turn = lax.fori_loop(0, NOBS // BATCH, batch, (anomalies, means, eye))
    high = turn.astype(BF16).astype(F32)
    low = (turn - high)[:, :MEMBERS]
    high = high[:, :MEMBERS]
    left = jnp.concatenate([high, high, low], axis=1).astype(BF16)

    def plane(p, _):
        start = p * (MEMBERS * 8)
        blocks = []
        for r in range(8):
            x = f_ref[pl.ds(start + r, MEMBERS, stride=8), :]
            big = x.astype(BF16)
            small = (x - big.astype(F32)).astype(BF16)
            blocks.append(jnp.concatenate([big, small, big], axis=0))
        for h in range(4):
            right = jnp.concatenate(blocks[2 * h : 2 * h + 2], axis=1)
            result = jnp.dot(left, right, preferred_element_type=F32)
            for i in range(2):
                turned[pl.ds(2 * h + i, MEMBERS, stride=8), :] = result[:, 128 * i : 128 * i + 128]
        out_ref[pl.ds(p * MEMBERS, MEMBERS)] = (
            turned[...].reshape(MEMBERS, 8, 128).astype(BF16)
        )
        return 0

    lax.fori_loop(0, PLANES, plane, 0)


def per_device(prior_state, courant, obs_tile, obs_site, obs_value, obs_var, loc_bits, batch_order):
    prior = prior_state.reshape(ROWS, 8, 128)
    wind = courant.reshape(2 * LEVELS, 8, 128)
    me = (lax.axis_index("lat") * N_LON + lax.axis_index("lon")).astype(jnp.int32)[None]
    dma = pltpu.SemaphoreType.DMA
    rows_shape = jax.ShapeDtypeStruct((2, ROWS, 128), BF16)
    cols_shape = jax.ShapeDtypeStruct((2, PLANES, 8, 128), BF16)
    obs_shape = jax.ShapeDtypeStruct((GROUP, 2, 128), F32)
    edge_rows, edge_cols = pl.pallas_call(
        edges_kernel,
        out_shape=(rows_shape, cols_shape),
        in_specs=[spec(VM)],
        out_specs=(spec(VM), spec(VM)),
        scratch_shapes=[VM((128, 128), F32)],
        name="edges",
    )(prior)
    halo_rows, halo_cols = pl.pallas_call(
        halo_kernel,
        out_shape=(rows_shape, cols_shape),
        in_specs=[spec(VM)] * 2,
        out_specs=(spec(VM), spec(VM)),
        scratch_shapes=[dma((4,)), dma((4,))],
        compiler_params=pltpu.CompilerParams(collective_id=0, has_side_effects=True),
        name="halo",
    )(edge_rows, edge_cols)
    forecast, contribution = pl.pallas_call(
        forecast_kernel,
        out_shape=(jax.ShapeDtypeStruct((ROWS * 8, 128), F32), obs_shape),
        in_specs=[spec(SM)] * 4 + [spec(VM)] * 4,
        out_specs=(spec(VM), spec(VM)),
        name="forecast",
    )(me, obs_tile, obs_site, batch_order, prior, wind, halo_rows, halo_cols)
    observed = pl.pallas_call(
        exchange_kernel,
        out_shape=obs_shape,
        in_specs=[spec(VM)],
        out_specs=spec(VM),
        scratch_shapes=[
            VM((GROUP, 2, 128), F32),
            VM((2, 128), F32),
            VM((N_Z, 2, 128), F32),
            VM((2, 128), F32),
            VM((GROUP, 2, 128), F32),
            dma((GROUP,)),
            dma((GROUP,)),
            dma((N_Z,)),
            dma((N_Z,)),
            dma((GROUP,)),
            dma((GROUP,)),
        ],
        compiler_params=pltpu.CompilerParams(collective_id=1, has_side_effects=True),
        name="exchange",
    )(contribution)
    bits = jnp.pad(loc_bits, ((0, 0), (0, 128 - loc_bits.shape[1])))
    analysis = pl.pallas_call(
        filter_kernel,
        out_shape=jax.ShapeDtypeStruct((ROWS, 8, 128), BF16),
        in_specs=[spec(SM)] * 6 + [spec(VM)] * 3,
        out_specs=spec(VM),
        scratch_shapes=[VM((128, 128), F32), VM((NOBS, 128), F32), VM((MEMBERS * 8, 128), F32)],
        name="filter",
    )(me, obs_tile, batch_order, obs_value, obs_var, loc_bits, bits, observed, forecast)
    return analysis.reshape(prior_state.shape)


def solution(mesh):
    placed = (
        P(None, None, None, "lat", "lon"),
        P(None, None, "lat", "lon"),
        P(),
        P(),
        P(),
        P(),
        P(),
        P(),
    )
    return jax.shard_map(
        per_device,
        mesh=mesh,
        in_specs=placed,
        out_specs=P(None, None, None, "lat", "lon"),
        check_vma=False,
    )
```

```python
import jax
import jax.numpy as jnp
from jax import lax
from jax.experimental import pallas as pl
from jax.experimental.pallas import tpu as pltpu
from jax.sharding import PartitionSpec as P

MESH = pl.DeviceIdType.MESH
EPSILON = 1e-05
MEMBERS = 80
PLANES = 8
LEVELS = 4
CELLS = 1024
NOBS = 64
BATCH = 16
N_LAT = 16
N_LON = 32
N_Z = 16
GROUP = 32
ROWS = PLANES * MEMBERS
F32 = jnp.float32
BF16 = jnp.bfloat16
VM = pltpu.VMEM
SM = pltpu.SMEM


def spec(space):
    return pl.BlockSpec(memory_space=space)


def exchange_kernel(
    tile_ref,
    site_ref,
    order_ref,
    prior_ref,
    wind_ref,
    f_ref,
    out_ref,
    wide,
    rows,
    edge_cols,
    halo_cols,
    mine_obs,
    got1,
    part,
    got2,
    total,
    halo_send,
    halo_recv,
    send,
    recv,
):
    lat = lax.axis_index("lat")
    lon = lax.axis_index("lon")
    z = lon // 2
    core = lax.rem(lon, 2)
    mine = lat * 2 + core
    me = lat * N_LON + lon
    north = (lax.rem(lat + 1, N_LAT), lon)
    south = (lax.rem(lat + N_LAT - 1, N_LAT), lon)
    east = (lat, lax.rem(lon + 1, N_LON))
    west = (lat, lax.rem(lon + N_LON - 1, N_LON))
    lane = lax.broadcasted_iota(jnp.int32, (8, 128), 1)
    sub = lax.broadcasted_iota(jnp.int32, (8, 128), 0)

    def other(d):
        return lax.rem(mine + d, GROUP)

    def group_id(n):
        return (n // 2, z * 2 + lax.rem(n, 2))

    def z_step(n):
        return 8 + ((n + 1) // 2) * (2 * lax.rem(n + 1, 2) - 1)

    def z_id(d):
        return (lat, lax.rem(z + d, N_Z) * 2 + core)

    def loop(first, count, body):
        lax.fori_loop(first, count, lambda d, c: (body(d), c)[1], 0)

    barrier = pltpu.get_barrier_semaphore()

    def greet(peer):
        pl.semaphore_signal(barrier, inc=1, device_id=peer, device_id_type=MESH)

    loop(0, N_Z - 1, lambda n: greet(z_id(z_step(n))))
    loop(1, GROUP, lambda d: greet(group_id(other(d))))
    greet(east)
    greet(west)

    lanes = lax.broadcasted_iota(jnp.int32, (MEMBERS, 128), 1)

    def edge_plane(p, acc):
        def block(g):
            for i in range(16):
                at = pl.multiple_of(g * 128 + i * 8, 8)
                wide[pl.ds(at, 8), :] = prior_ref[p * MEMBERS + g * 16 + i].astype(F32)
            for r in range(8):
                part_rows = wide[pl.ds(g * 128 + r, 16, stride=8), :]
                rows[p, r + 1, pl.ds(pl.multiple_of(g * 16, 16), 16), :] = part_rows.astype(BF16)

        loop(0, 5, block)
        first, last = acc
        for r in range(8):
            x = rows[p, r + 1].astype(F32)
            here = lanes == p * 8 + r
            first = jnp.where(here, pltpu.roll(x, p * 8 + r, 1), first)
            last = jnp.where(here, pltpu.roll(x, p * 8 + r + 1, 1), last)
        return first, last

    zero = jnp.zeros((MEMBERS, 128), F32)
    first, last = lax.fori_loop(0, PLANES, edge_plane, (zero, zero))
    edge_cols[0] = last.astype(BF16)
    edge_cols[1] = first.astype(BF16)

    halves = []
    for h in range(2):
        owned = jnp.int32(0)
        for n in range(32):
            q = 32 * h + n
            k = order_ref[q // BATCH] * BATCH + q % BATCH
            hit = (tile_ref[k] == me).astype(jnp.int32)
            owned = owned | (hit << n)
        halves.append(owned)

    pl.semaphore_wait(barrier, GROUP - 1 + N_Z - 1 + 2)
    halos = []
    for n, (src, dst, peer) in enumerate(
        (
            (rows.at[:, 8], rows.at[:, 0], north),
            (rows.at[:, 1], rows.at[:, 9], south),
            (edge_cols.at[0], halo_cols.at[0], east),
            (edge_cols.at[1], halo_cols.at[1], west),
        )
    ):
        copy = pltpu.make_async_remote_copy(
            src_ref=src,
            dst_ref=dst,
            send_sem=halo_send.at[n],
            recv_sem=halo_recv.at[n],
            device_id=peer,
            device_id_type=MESH,
        )
        copy.start()
        halos.append(copy)
    for copy in halos:
        copy.wait_recv()

    has_south = (lat > 0).astype(F32)
    has_north = (lat < N_LAT - 1).astype(F32)
    for p in range(PLANES):
        rows[p, 0] = (rows[p, 0].astype(F32) * has_south).astype(BF16)
        rows[p, 9] = (rows[p, 9].astype(F32) * has_north).astype(BF16)
    fill = jnp.zeros((128 - MEMBERS, 128), BF16)
    place = lax.broadcasted_iota(jnp.int32, (NOBS, 128), 0)

    def slot(n, carry):
        lo, hi, table = carry
        use_hi = lo == 0
        word = jnp.where(use_hi, hi, lo)
        low = word & (-word)
        q = jnp.int32(0)
        for bit, pattern in enumerate(
            (-1431655766, -858993460, -252645136, -16711936, -65536)
        ):
            q = q + jnp.where((low & jnp.int32(pattern)) != 0, 1 << bit, 0)
        q = q + jnp.where(use_hi, 32, 0)
        spot = jnp.where(word == 0, NOBS, q)
        lo_next = jnp.where(use_hi, lo, lo & (lo - 1))
        hi_next = jnp.where(use_hi, hi & (hi - 1), hi)
        k = order_ref[q // BATCH] * BATCH + q % BATCH
        s = site_ref[k]
        p = s // CELLS
        r = (s // 128) % 8
        c = s % 128
        around = jnp.concatenate(
            [rows[p, r + 1], fill, rows[p, r], fill, rows[p, r + 2], fill], axis=0
        )
        shift = jnp.where(sub == 1, -1, jnp.where(sub == 2, 1, 0))
        pick = (lane == c + shift).astype(BF16)
        found = lax.dot_general(
            pick, around, (((1,), (1,)), ((), ())), preferred_element_type=F32
        )
        sides = jnp.concatenate([halo_cols[0], fill, halo_cols[1], fill], axis=0)
        beside = lax.dot_general(
            (lane == p * 8 + r).astype(BF16),
            sides,
            (((1,), (1,)), ((), ())),
            preferred_element_type=F32,
        )
        at_cell = (sub == r) & (lane == c)
        level = p % LEVELS
        cu = jnp.sum(jnp.where(at_cell, wind_ref[level], 0.0), axis=0, keepdims=True)
        cv = jnp.sum(jnp.where(at_cell, wind_ref[LEVELS + level], 0.0), axis=0, keepdims=True)
        cu = jnp.sum(cu, axis=1, keepdims=True)
        cv = jnp.sum(cv, axis=1, keepdims=True)
        x = found[0:1, 0:128]
        column = jnp.full((1, 128), c, jnp.int32)
        xw = jnp.where(column == 0, beside[0:1, 0:128], found[1:2, 0:128])
        xe = jnp.where(column == 127, beside[0:1, 128:256], found[2:3, 0:128])
        xs = found[0:1, 128:256]
        xn = found[0:1, 256:384]
        f = (
            x
            - jnp.maximum(cu, 0.0) * (x - xw)
            - jnp.minimum(cu, 0.0) * (xe - x)
            - jnp.maximum(cv, 0.0) * (x - xs)
            - jnp.minimum(cv, 0.0) * (xn - x)
        )
        table = jnp.where(place == spot, f, table)
        return lo_next, hi_next, table

    _, _, table = lax.fori_loop(
        0, BATCH, slot, (halves[0], halves[1], jnp.zeros((NOBS, 128), F32))
    )
    for n in range(GROUP):
        mine_obs[n] = table[2 * n : 2 * n + 2, :]

    def copy1(dst, slot_id):
        return pltpu.make_async_remote_copy(
            src_ref=mine_obs.at[dst],
            dst_ref=got1.at[slot_id],
            send_sem=send.at[0],
            recv_sem=recv.at[0],
            device_id=group_id(dst),
            device_id_type=MESH,
        )

    def copy2(d):
        return pltpu.make_async_remote_copy(
            src_ref=part,
            dst_ref=got2.at[d],
            send_sem=send.at[1],
            recv_sem=recv.at[1],
            device_id=z_id(d),
            device_id_type=MESH,
        )

    def copy3(dst):
        return pltpu.make_async_remote_copy(
            src_ref=total,
            dst_ref=out_ref.at[mine],
            send_sem=send.at[2],
            recv_sem=recv.at[2],
            device_id=group_id(dst),
            device_id_type=MESH,
        )

    def bulk(buffer, count, n):
        return pltpu.make_async_remote_copy(
            src_ref=buffer.at[pl.ds(0, count)],
            dst_ref=buffer.at[pl.ds(0, count)],
            send_sem=send.at[n],
            recv_sem=recv.at[n],
            device_id=north,
            device_id_type=MESH,
        )

    lane16 = lax.broadcasted_iota(jnp.int32, (16, 128), 1)

    def forecast(p):
        level = lax.rem(p, LEVELS)
        for r in range(8):
            cu = wind_ref[level, r : r + 1, :]
            cv = wind_ref[LEVELS + level, r : r + 1, :]
            cu_up, cu_dn = jnp.maximum(cu, 0.0), jnp.minimum(cu, 0.0)
            cv_up, cv_dn = jnp.maximum(cv, 0.0), jnp.minimum(cv, 0.0)
            spot = p * 8 + r
            cells = slice(128 * r, 128 * r + 128)
            for g in range(5):
                some = slice(16 * g, 16 * g + 16)
                x = rows[p, r + 1, some, :].astype(F32)
                xs = rows[p, r, some, :].astype(F32)
                xn = rows[p, r + 2, some, :].astype(F32)
                from_west = halo_cols[0, some, :].astype(F32)
                from_east = halo_cols[1, some, :].astype(F32)
                xw = jnp.where(
                    lane16 == 0,
                    pltpu.roll(from_west, lax.rem(128 - spot, 128), 1),
                    pltpu.roll(x, 1, 1),
                )
                xe = jnp.where(
                    lane16 == 127, pltpu.roll(from_east, 127 - spot, 1), pltpu.roll(x, 127, 1)
                )
                f = (
                    x
                    - cu_up * (x - xw)
                    - cu_dn * (xe - x)
                    - cv_up * (x - xs)
                    - cv_dn * (xn - x)
                )
                big = f.astype(BF16)
                f_ref[p, some, cells] = big
                low = slice(MEMBERS + 16 * g, MEMBERS + 16 * g + 16)
                f_ref[p, low, cells] = (f - big.astype(F32)).astype(BF16)

    loop(1, GROUP, lambda d: copy1(other(d), d).start())
    loop(0, 2, forecast)
    bulk(got1, GROUP - 1, 0).wait_recv()
    acc = mine_obs[mine]
    for d in range(1, GROUP):
        acc = acc + got1[d]
    part[...] = acc
    loop(0, N_Z - 1, lambda n: copy2(z_step(n)).start())
    loop(2, 6, forecast)
    bulk(got2, N_Z - 1, 1).wait_recv()
    acc = part[...]
    for d in range(1, N_Z):
        acc = acc + got2[d]
    total[...] = acc
    loop(1, GROUP, lambda d: copy3(other(d)).start())
    out_ref[mine] = acc
    loop(6, PLANES, forecast)
    bulk(out_ref, GROUP - 1, 2).wait_recv()
    for copy in halos:
        copy.wait_send()
    bulk(got1, GROUP - 1, 0).wait_send()
    bulk(got2, N_Z - 1, 1).wait_send()
    bulk(got1, GROUP - 1, 2).wait_send()


def filter_kernel(
    me_ref,
    tile_ref,
    order_ref,
    value_ref,
    var_ref,
    bits_ref,
    obs_ref,
    f_ref,
    out_ref,
    table,
    mask_ref,
    own_ref,
    turned,
):
    me = me_ref[0]
    for n in range(GROUP):
        table[2 * n : 2 * n + 2, :] = obs_ref[n]
    table[NOBS:, :] = jnp.zeros((128 - NOBS, 128), F32)
    lane = lax.broadcasted_iota(jnp.int32, (1, 128), 1)

    def put(q, row):
        k = order_ref[q // BATCH] * BATCH + lax.rem(q, BATCH)
        return jnp.where(lane == q, tile_ref[k], row)

    owners = lax.fori_loop(0, NOBS, put, jnp.zeros((1, 128), jnp.int32))
    word_of = owners // 30
    bit_of = owners - word_of * 30
    own_word = me // 30
    words = bits_ref[...]
    chosen = jnp.zeros((NOBS, 128), jnp.int32)
    chosen_own = jnp.zeros((NOBS, 128), jnp.int32)
    for w in range(18):
        word = jnp.broadcast_to(words[:, w : w + 1], (NOBS, 128))
        chosen = jnp.where(word_of == w, word, chosen)
        chosen_own = jnp.where(own_word == w, word, chosen_own)
    scale = 1.0 / (MEMBERS - 1)
    mask_ref[...] = jnp.bitwise_and(jnp.right_shift(chosen, bit_of), 1).astype(F32) * scale
    own_bit = jnp.full((NOBS, 128), lax.rem(me, 30), jnp.int32)
    own_ref[...] = jnp.bitwise_and(jnp.right_shift(chosen_own, own_bit), 1).astype(F32) * scale
    state = jnp.transpose(table[...])[:MEMBERS, :]
    means = jnp.sum(state, axis=0, keepdims=True) * (1.0 / MEMBERS)
    anomalies = state - means
    eye = (
        lax.broadcasted_iota(jnp.int32, (MEMBERS, 128), 0)
        == lax.broadcasted_iota(jnp.int32, (MEMBERS, 128), 1)
    ).astype(F32)

    def batch(b, carry):
        anomalies, means, turn = carry
        base = order_ref[b] * BATCH
        for j in range(BATCH):
            k = base + j
            r = var_ref[k]
            val = value_ref[k]
            own = own_ref[pl.ds(k, 1), :]
            row = mask_ref[pl.ds(k, 1), :]
            a = jnp.broadcast_to(anomalies[:, j : j + 1], (MEMBERS, 128))
            m = jnp.broadcast_to(means[:, j : j + 1], (1, 128))
            v = jnp.sum(a * a, axis=0, keepdims=True) * (1.0 / (MEMBERS - 1)) + EPSILON
            cov = jnp.sum(anomalies * a, axis=0, keepdims=True) * row
            cov_own = jnp.sum(turn * a, axis=0, keepdims=True) * own
            whole = v + r
            shrink = 1.0 / (whole + jnp.sqrt(r * whole))
            shift = (val - m) / whole
            anomalies = anomalies - (cov * shrink) * a
            means = means + cov * shift
            turn = turn + cov_own * (shift - shrink * a)
        mask_ref[...] = pltpu.roll(mask_ref[...], 128 - BATCH, 1)
        return (
            pltpu.roll(anomalies, 128 - BATCH, 1),
            pltpu.roll(means, 128 - BATCH, 1),
            turn,
        )

    _, _, turn = lax.fori_loop(0, NOBS // BATCH, batch, (anomalies, means, eye))
    high = turn.astype(BF16).astype(F32)
    low = (turn - high)[:, :MEMBERS]
    high = high[:, :MEMBERS]
    left = jnp.concatenate([high, high, low], axis=1).astype(BF16)

    def plane(p, _):
        for h in range(4):
            cells = slice(256 * h, 256 * h + 256)
            right = jnp.concatenate([f_ref[p, :, cells], f_ref[p, :MEMBERS, cells]], axis=0)
            result = jnp.dot(left, right, preferred_element_type=F32)
            for i in range(2):
                turned[pl.ds(2 * h + i, MEMBERS, stride=8), :] = result[:, 128 * i : 128 * i + 128]
        out_ref[pl.ds(p * MEMBERS, MEMBERS)] = (
            turned[...].reshape(MEMBERS, 8, 128).astype(BF16)
        )
        return 0

    lax.fori_loop(0, PLANES, plane, 0)


def per_device(prior_state, courant, obs_tile, obs_site, obs_value, obs_var, loc_bits, batch_order):
    prior = prior_state.reshape(ROWS, 8, 128)
    wind = courant.reshape(2 * LEVELS, 8, 128)
    me = (lax.axis_index("lat") * N_LON + lax.axis_index("lon")).astype(jnp.int32)[None]
    dma = pltpu.SemaphoreType.DMA
    forecast, observed = pl.pallas_call(
        exchange_kernel,
        out_shape=(
            jax.ShapeDtypeStruct((PLANES, 2 * MEMBERS, CELLS), BF16),
            jax.ShapeDtypeStruct((GROUP, 2, 128), F32),
        ),
        in_specs=[spec(SM)] * 3 + [spec(VM)] * 2,
        out_specs=(spec(VM), spec(VM)),
        scratch_shapes=[
            VM((MEMBERS * 8, 128), F32),
            VM((PLANES, 10, MEMBERS, 128), BF16),
            VM((2, MEMBERS, 128), BF16),
            VM((2, MEMBERS, 128), BF16),
            VM((GROUP, 2, 128), F32),
            VM((GROUP, 2, 128), F32),
            VM((2, 128), F32),
            VM((N_Z, 2, 128), F32),
            VM((2, 128), F32),
            dma((4,)),
            dma((4,)),
            dma((3,)),
            dma((3,)),
        ],
        compiler_params=pltpu.CompilerParams(collective_id=0, has_side_effects=True),
        name="exchange",
    )(obs_tile, obs_site, batch_order, prior, wind)
    analysis = pl.pallas_call(
        filter_kernel,
        out_shape=jax.ShapeDtypeStruct((ROWS, 8, 128), BF16),
        in_specs=[spec(SM)] * 5 + [spec(VM)] * 3,
        out_specs=spec(VM),
        scratch_shapes=[
            VM((128, 128), F32),
            VM((NOBS, 128), F32),
            VM((NOBS, 128), F32),
            VM((MEMBERS * 8, 128), F32),
        ],
        name="filter",
    )(me, obs_tile, batch_order, obs_value, obs_var, loc_bits, observed, forecast)
    return analysis.reshape(prior_state.shape)


def solution(mesh):
    placed = (
        P(None, None, None, "lat", "lon"),
        P(None, None, "lat", "lon"),
        P(),
        P(),
        P(),
        P(),
        P(),
        P(),
    )
    return jax.shard_map(
        per_device,
        mesh=mesh,
        in_specs=placed,
        out_specs=P(None, None, None, "lat", "lon"),
        check_vma=False,
    )
```

```python
import jax
import jax.numpy as jnp
from jax import lax
from jax.experimental import pallas as pl
from jax.experimental.pallas import tpu as pltpu
from jax.sharding import PartitionSpec as P

MESH = pl.DeviceIdType.MESH
EPSILON = 1e-05
MEMBERS = 80
PLANES = 8
LEVELS = 4
CELLS = 1024
NOBS = 64
BATCH = 16
N_LAT = 16
N_LON = 32
N_Z = 16
GROUP = 32
ROWS = PLANES * MEMBERS
F32 = jnp.float32
BF16 = jnp.bfloat16
VM = pltpu.VMEM
SM = pltpu.SMEM


def spec(space):
    return pl.BlockSpec(memory_space=space)


def exchange_kernel(
    tile_ref,
    site_ref,
    order_ref,
    prior_hbm,
    wind_ref,
    bits_ref,
    f_hbm,
    out_ref,
    mask_ref,
    prior_ref,
    f_ref,
    wide,
    rows,
    edge_cols,
    halo_cols,
    mine_obs,
    got1,
    part,
    got2,
    total,
    halo_send,
    halo_recv,
    send,
    recv,
    load_sem,
    store_sem,
):
    lat = lax.axis_index("lat")
    lon = lax.axis_index("lon")
    z = lon // 2
    core = lax.rem(lon, 2)
    mine = lat * 2 + core
    me = lat * N_LON + lon
    north = (lax.rem(lat + 1, N_LAT), lon)
    south = (lax.rem(lat + N_LAT - 1, N_LAT), lon)
    east = (lat, lax.rem(lon + 1, N_LON))
    west = (lat, lax.rem(lon + N_LON - 1, N_LON))
    lane = lax.broadcasted_iota(jnp.int32, (8, 128), 1)
    sub = lax.broadcasted_iota(jnp.int32, (8, 128), 0)

    def other(d):
        return lax.rem(mine + d, GROUP)

    def group_id(n):
        return (n // 2, z * 2 + lax.rem(n, 2))

    def z_step(n):
        return 8 + ((n + 1) // 2) * (2 * lax.rem(n + 1, 2) - 1)

    def z_id(d):
        return (lat, lax.rem(z + d, N_Z) * 2 + core)

    def loop(first, count, body):
        lax.fori_loop(first, count, lambda d, c: (body(d), c)[1], 0)

    load = pltpu.make_async_copy(prior_hbm, prior_ref, load_sem)
    load.start()
    barrier = pltpu.get_barrier_semaphore()

    def greet(peer):
        pl.semaphore_signal(barrier, inc=1, device_id=peer, device_id_type=MESH)

    loop(0, N_Z - 1, lambda n: greet(z_id(z_step(n))))
    loop(1, GROUP, lambda d: greet(group_id(other(d))))
    greet(east)
    greet(west)
    load.wait()

    lanes = lax.broadcasted_iota(jnp.int32, (MEMBERS, 128), 1)

    def edge_plane(p, acc):
        def block(g):
            for i in range(16):
                at = pl.multiple_of(g * 128 + i * 8, 8)
                wide[pl.ds(at, 8), :] = prior_ref[p * MEMBERS + g * 16 + i].astype(F32)
            for r in range(8):
                part_rows = wide[pl.ds(g * 128 + r, 16, stride=8), :]
                rows[p, r + 1, pl.ds(pl.multiple_of(g * 16, 16), 16), :] = part_rows.astype(BF16)

        loop(0, 5, block)
        first, last = acc
        for r in range(8):
            x = rows[p, r + 1].astype(F32)
            here = lanes == p * 8 + r
            first = jnp.where(here, pltpu.roll(x, p * 8 + r, 1), first)
            last = jnp.where(here, pltpu.roll(x, p * 8 + r + 1, 1), last)
        return first, last

    zero = jnp.zeros((MEMBERS, 128), F32)
    first, last = lax.fori_loop(0, PLANES, edge_plane, (zero, zero))
    edge_cols[0] = last.astype(BF16)
    edge_cols[1] = first.astype(BF16)

    halves = []
    for h in range(2):
        owned = jnp.int32(0)
        for n in range(32):
            q = 32 * h + n
            k = order_ref[q // BATCH] * BATCH + q % BATCH
            hit = (tile_ref[k] == me).astype(jnp.int32)
            owned = owned | (hit << n)
        halves.append(owned)

    pl.semaphore_wait(barrier, GROUP - 1 + N_Z - 1 + 2)
    halos = []
    for n, (src, dst, peer) in enumerate(
        (
            (rows.at[:, 8], rows.at[:, 0], north),
            (rows.at[:, 1], rows.at[:, 9], south),
            (edge_cols.at[0], halo_cols.at[0], east),
            (edge_cols.at[1], halo_cols.at[1], west),
        )
    ):
        copy = pltpu.make_async_remote_copy(
            src_ref=src,
            dst_ref=dst,
            send_sem=halo_send.at[n],
            recv_sem=halo_recv.at[n],
            device_id=peer,
            device_id_type=MESH,
        )
        copy.start()
        halos.append(copy)
    for copy in halos:
        copy.wait_recv()

    has_south = (lat > 0).astype(F32)
    has_north = (lat < N_LAT - 1).astype(F32)
    for p in range(PLANES):
        rows[p, 0] = (rows[p, 0].astype(F32) * has_south).astype(BF16)
        rows[p, 9] = (rows[p, 9].astype(F32) * has_north).astype(BF16)
    fill = jnp.zeros((128 - MEMBERS, 128), BF16)
    place = lax.broadcasted_iota(jnp.int32, (NOBS, 128), 0)

    def slot(carry):
        lo, hi, table = carry
        use_hi = lo == 0
        word = jnp.where(use_hi, hi, lo)
        low = word & (-word)
        q = jnp.int32(0)
        for bit, pattern in enumerate(
            (-1431655766, -858993460, -252645136, -16711936, -65536)
        ):
            q = q + jnp.where((low & jnp.int32(pattern)) != 0, 1 << bit, 0)
        q = q + jnp.where(use_hi, 32, 0)
        spot = jnp.where(word == 0, NOBS, q)
        lo_next = jnp.where(use_hi, lo, lo & (lo - 1))
        hi_next = jnp.where(use_hi, hi & (hi - 1), hi)
        k = order_ref[q // BATCH] * BATCH + q % BATCH
        s = site_ref[k]
        p = s // CELLS
        r = (s // 128) % 8
        c = s % 128
        around = jnp.concatenate(
            [rows[p, r + 1], fill, rows[p, r], fill, rows[p, r + 2], fill], axis=0
        )
        shift = jnp.where(sub == 1, -1, jnp.where(sub == 2, 1, 0))
        pick = (lane == c + shift).astype(BF16)
        found = lax.dot_general(
            pick, around, (((1,), (1,)), ((), ())), preferred_element_type=F32
        )
        sides = jnp.concatenate([halo_cols[0], fill, halo_cols[1], fill], axis=0)
        beside = lax.dot_general(
            (lane == p * 8 + r).astype(BF16),
            sides,
            (((1,), (1,)), ((), ())),
            preferred_element_type=F32,
        )
        at_cell = (sub == r) & (lane == c)
        level = p % LEVELS
        cu = jnp.sum(jnp.where(at_cell, wind_ref[level], 0.0), axis=0, keepdims=True)
        cv = jnp.sum(jnp.where(at_cell, wind_ref[LEVELS + level], 0.0), axis=0, keepdims=True)
        cu = jnp.sum(cu, axis=1, keepdims=True)
        cv = jnp.sum(cv, axis=1, keepdims=True)
        x = found[0:1, 0:128]
        column = jnp.full((1, 128), c, jnp.int32)
        xw = jnp.where(column == 0, beside[0:1, 0:128], found[1:2, 0:128])
        xe = jnp.where(column == 127, beside[0:1, 128:256], found[2:3, 0:128])
        xs = found[0:1, 128:256]
        xn = found[0:1, 256:384]
        f = (
            x
            - jnp.maximum(cu, 0.0) * (x - xw)
            - jnp.minimum(cu, 0.0) * (xe - x)
            - jnp.maximum(cv, 0.0) * (x - xs)
            - jnp.minimum(cv, 0.0) * (xn - x)
        )
        table = jnp.where(place == spot, f, table)
        return lo_next, hi_next, table

    def slots(n, carry):
        for _ in range(4):
            carry = slot(carry)
        return carry

    _, _, table = lax.fori_loop(
        0, BATCH // 4, slots, (halves[0], halves[1], jnp.zeros((NOBS, 128), F32))
    )
    for n in range(GROUP):
        mine_obs[n] = table[2 * n : 2 * n + 2, :]

    def copy1(dst, slot_id):
        return pltpu.make_async_remote_copy(
            src_ref=mine_obs.at[dst],
            dst_ref=got1.at[slot_id],
            send_sem=send.at[0],
            recv_sem=recv.at[0],
            device_id=group_id(dst),
            device_id_type=MESH,
        )

    def copy2(d):
        return pltpu.make_async_remote_copy(
            src_ref=part,
            dst_ref=got2.at[d],
            send_sem=send.at[1],
            recv_sem=recv.at[1],
            device_id=z_id(d),
            device_id_type=MESH,
        )

    def copy3(dst):
        return pltpu.make_async_remote_copy(
            src_ref=total,
            dst_ref=out_ref.at[mine],
            send_sem=send.at[2],
            recv_sem=recv.at[2],
            device_id=group_id(dst),
            device_id_type=MESH,
        )

    def bulk(buffer, count, n):
        return pltpu.make_async_remote_copy(
            src_ref=buffer.at[pl.ds(0, count)],
            dst_ref=buffer.at[pl.ds(0, count)],
            send_sem=send.at[n],
            recv_sem=recv.at[n],
            device_id=north,
            device_id_type=MESH,
        )

    lane16 = lax.broadcasted_iota(jnp.int32, (16, 128), 1)

    def store(p):
        return pltpu.make_async_copy(f_ref.at[p], f_hbm.at[p], store_sem.at[p])

    def forecast(p):
        level = lax.rem(p, LEVELS)
        for r in range(8):
            cu = wind_ref[level, r : r + 1, :]
            cv = wind_ref[LEVELS + level, r : r + 1, :]
            cu_up, cu_dn = jnp.maximum(cu, 0.0), jnp.minimum(cu, 0.0)
            cv_up, cv_dn = jnp.maximum(cv, 0.0), jnp.minimum(cv, 0.0)
            spot = p * 8 + r
            cells = slice(128 * r, 128 * r + 128)
            for g in range(5):
                some = slice(16 * g, 16 * g + 16)
                x = rows[p, r + 1, some, :].astype(F32)
                xs = rows[p, r, some, :].astype(F32)
                xn = rows[p, r + 2, some, :].astype(F32)
                from_west = halo_cols[0, some, :].astype(F32)
                from_east = halo_cols[1, some, :].astype(F32)
                xw = jnp.where(
                    lane16 == 0,
                    pltpu.roll(from_west, lax.rem(128 - spot, 128), 1),
                    pltpu.roll(x, 1, 1),
                )
                xe = jnp.where(
                    lane16 == 127, pltpu.roll(from_east, 127 - spot, 1), pltpu.roll(x, 127, 1)
                )
                f = (
                    x
                    - cu_up * (x - xw)
                    - cu_dn * (xe - x)
                    - cv_up * (x - xs)
                    - cv_dn * (xn - x)
                )
                big = f.astype(BF16)
                f_ref[p, some, cells] = big
                low = slice(MEMBERS + 16 * g, MEMBERS + 16 * g + 16)
                f_ref[p, low, cells] = (f - big.astype(F32)).astype(BF16)
        store(p).start()

    def masks():
        owner = jnp.zeros((NOBS, 128), jnp.int32)
        for q in range(NOBS):
            k = order_ref[q // BATCH] * BATCH + q % BATCH
            owner = jnp.where(place == q, tile_ref[k], owner)
        word_of = owner // 30
        bit_of = owner - word_of * 30
        own_word = me // 30
        own_bit = jnp.full((8, NOBS), lax.rem(me, 30), jnp.int32)
        chosen = jnp.zeros((NOBS, NOBS), jnp.int32)
        own = jnp.zeros((8, NOBS), jnp.int32)
        for w in range(18):
            word = bits_ref[w : w + 1, :]
            chosen = jnp.where(word_of[:, :NOBS] == w, word, chosen)
            own = jnp.where(jnp.full((8, NOBS), own_word, jnp.int32) == w, word, own)
        scale = 1.0 / (MEMBERS - 1)
        hit = jnp.bitwise_and(jnp.right_shift(chosen, bit_of[:, :NOBS]), 1)
        own_hit = jnp.bitwise_and(jnp.right_shift(own, own_bit), 1)
        mask_ref[:NOBS, :] = hit.astype(F32) * scale
        mask_ref[NOBS:, :] = own_hit.astype(F32) * scale

    loop(1, GROUP, lambda d: copy1(other(d), d).start())
    loop(0, 2, forecast)
    bulk(got1, GROUP - 1, 0).wait_recv()
    acc = mine_obs[mine]
    for d in range(1, GROUP):
        acc = acc + got1[d]
    part[...] = acc
    loop(0, N_Z - 1, lambda n: copy2(z_step(n)).start())
    masks()
    loop(2, 6, forecast)
    bulk(got2, N_Z - 1, 1).wait_recv()
    acc = part[...]
    for d in range(1, N_Z):
        acc = acc + got2[d]
    total[...] = acc
    loop(1, GROUP, lambda d: copy3(other(d)).start())
    out_ref[mine] = acc
    loop(6, PLANES, forecast)
    bulk(out_ref, GROUP - 1, 2).wait_recv()
    for copy in halos:
        copy.wait_send()
    for p in range(PLANES):
        store(p).wait()
    bulk(got1, GROUP - 1, 0).wait_send()
    bulk(got2, N_Z - 1, 1).wait_send()
    bulk(got1, GROUP - 1, 2).wait_send()


def filter_kernel(
    order_ref,
    value_ref,
    var_ref,
    bits_ref,
    obs_ref,
    f_hbm,
    out_hbm,
    table,
    mask_ref,
    own_ref,
    turned,
    f_ref,
    out_ref,
    load_sem,
    store_sem,
):
    load = pltpu.make_async_copy(f_hbm, f_ref, load_sem)
    load.start()
    for n in range(GROUP):
        table[2 * n : 2 * n + 2, :] = obs_ref[n]
    table[NOBS:, :] = jnp.zeros((128 - NOBS, 128), F32)
    state = jnp.transpose(table[...])[:MEMBERS, :]
    table[...] = jnp.zeros((128, 128), F32)
    table[: NOBS + 8, :NOBS] = bits_ref[...]
    masks = jnp.transpose(table[...])[:NOBS, :]
    mask_ref[...] = masks
    own_ref[...] = jnp.broadcast_to(masks[:, NOBS : NOBS + 1], (NOBS, 128))
    means = jnp.sum(state, axis=0, keepdims=True) * (1.0 / MEMBERS)
    anomalies = state - means
    eye = (
        lax.broadcasted_iota(jnp.int32, (MEMBERS, 128), 0)
        == lax.broadcasted_iota(jnp.int32, (MEMBERS, 128), 1)
    ).astype(F32)

    def spread(x, j):
        return jnp.broadcast_to(x[:, j : j + 1], (x.shape[0], 128))

    def total(x):
        return jnp.sum(x, axis=0, keepdims=True)

    def batch(b, carry):
        anomalies, means, turn = carry
        base = order_ref[b] * BATCH
        a = spread(anomalies, 0)
        m = spread(means, 0)
        for j in range(BATCH):
            k = base + j
            r = var_ref[k]
            val = value_ref[k]
            own = own_ref[pl.ds(k, 1), :]
            row = mask_ref[pl.ds(k, 1), :]
            whole = total(a * a) * (1.0 / (MEMBERS - 1)) + (r + EPSILON)
            shrink = 1.0 / (whole + jnp.sqrt(r * whole))
            shift = (val - m) / whole
            if j + 1 < BATCH:
                after = spread(anomalies, j + 1)
                link = total(after * a) * spread(row, j + 1)
                a_next = after - (link * shrink) * a
                m_next = spread(means, j + 1) + link * shift
            cov = total(anomalies * a) * row
            cov_own = total(turn * a) * own
            anomalies = anomalies - (cov * shrink) * a
            means = means + cov * shift
            turn = turn + cov_own * (shift - shrink * a)
            if j + 1 < BATCH:
                a, m = a_next, m_next
        mask_ref[...] = pltpu.roll(mask_ref[...], 128 - BATCH, 1)
        return (
            pltpu.roll(anomalies, 128 - BATCH, 1),
            pltpu.roll(means, 128 - BATCH, 1),
            turn,
        )

    _, _, turn = lax.fori_loop(0, NOBS // BATCH, batch, (anomalies, means, eye))
    high = turn.astype(BF16).astype(F32)
    low = (turn - high)[:, :MEMBERS]
    high = high[:, :MEMBERS]
    left = jnp.concatenate([high, high, low], axis=1).astype(BF16)
    load.wait()

    def store(p):
        block = pl.ds(p * MEMBERS, MEMBERS)
        return pltpu.make_async_copy(out_ref.at[block], out_hbm.at[block], store_sem.at[p])

    def plane(p, _):
        for h in range(4):
            cells = slice(256 * h, 256 * h + 256)
            right = jnp.concatenate([f_ref[p, :, cells], f_ref[p, :MEMBERS, cells]], axis=0)
            result = jnp.dot(left, right, preferred_element_type=F32)
            for i in range(2):
                turned[pl.ds(2 * h + i, MEMBERS, stride=8), :] = result[:, 128 * i : 128 * i + 128]
        out_ref[pl.ds(p * MEMBERS, MEMBERS)] = (
            turned[...].reshape(MEMBERS, 8, 128).astype(BF16)
        )
        store(p).start()
        return 0

    lax.fori_loop(0, PLANES, plane, 0)
    for p in range(PLANES):
        store(p).wait()


def per_device(prior_state, courant, obs_tile, obs_site, obs_value, obs_var, loc_bits, batch_order):
    prior = prior_state.reshape(ROWS, 8, 128)
    wind = courant.reshape(2 * LEVELS, 8, 128)
    dma = pltpu.SemaphoreType.DMA
    forecast, observed, masks = pl.pallas_call(
        exchange_kernel,
        out_shape=(
            jax.ShapeDtypeStruct((PLANES, 2 * MEMBERS, CELLS), BF16),
            jax.ShapeDtypeStruct((GROUP, 2, 128), F32),
            jax.ShapeDtypeStruct((NOBS + 8, NOBS), F32),
        ),
        in_specs=[spec(SM)] * 3 + [spec(pl.ANY)] + [spec(VM)] * 2,
        out_specs=(spec(pl.ANY), spec(VM), spec(VM)),
        scratch_shapes=[
            VM((ROWS, 8, 128), BF16),
            VM((PLANES, 2 * MEMBERS, CELLS), BF16),
            VM((MEMBERS * 8, 128), F32),
            VM((PLANES, 10, MEMBERS, 128), BF16),
            VM((2, MEMBERS, 128), BF16),
            VM((2, MEMBERS, 128), BF16),
            VM((GROUP, 2, 128), F32),
            VM((GROUP, 2, 128), F32),
            VM((2, 128), F32),
            VM((N_Z, 2, 128), F32),
            VM((2, 128), F32),
            dma((4,)),
            dma((4,)),
            dma((3,)),
            dma((3,)),
            dma,
            dma((PLANES,)),
        ],
        compiler_params=pltpu.CompilerParams(collective_id=0, has_side_effects=True),
        name="exchange",
    )(obs_tile, obs_site, batch_order, prior, wind, loc_bits.T)
    analysis = pl.pallas_call(
        filter_kernel,
        out_shape=jax.ShapeDtypeStruct((ROWS, 8, 128), BF16),
        in_specs=[spec(SM)] * 3 + [spec(VM)] * 2 + [spec(pl.ANY)],
        out_specs=spec(pl.ANY),
        scratch_shapes=[
            VM((128, 128), F32),
            VM((NOBS, 128), F32),
            VM((NOBS, 128), F32),
            VM((MEMBERS * 8, 128), F32),
            VM((PLANES, 2 * MEMBERS, CELLS), BF16),
            VM((ROWS, 8, 128), BF16),
            dma,
            dma((PLANES,)),
        ],
        name="filter",
    )(batch_order, obs_value, obs_var, masks, observed, forecast)
    return analysis.reshape(prior_state.shape)


def solution(mesh):
    placed = (
        P(None, None, None, "lat", "lon"),
        P(None, None, "lat", "lon"),
        P(),
        P(),
        P(),
        P(),
        P(),
        P(),
    )
    return jax.shard_map(
        per_device,
        mesh=mesh,
        in_specs=placed,
        out_specs=P(None, None, None, "lat", "lon"),
        check_vma=False,
    )
```

```python
import jax
import jax.numpy as jnp
from jax import lax
from jax.experimental import pallas as pl
from jax.experimental.pallas import tpu as pltpu
from jax.sharding import PartitionSpec as P

MESH = pl.DeviceIdType.MESH
EPSILON = 1e-05
MEMBERS = 80
PLANES = 8
LEVELS = 4
CELLS = 1024
NOBS = 64
BATCH = 16
N_LAT = 16
N_LON = 32
N_Z = 16
GROUP = 32
ROWS = PLANES * MEMBERS
F32 = jnp.float32
BF16 = jnp.bfloat16
VM = pltpu.VMEM
SM = pltpu.SMEM


def spec(space):
    return pl.BlockSpec(memory_space=space)


def exchange_kernel(
    tile_ref,
    site_ref,
    order_ref,
    prior_hbm,
    wind_ref,
    bits_ref,
    f_hbm,
    out_ref,
    mask_ref,
    prior_ref,
    f_ref,
    wide,
    rows,
    edge_cols,
    halo_cols,
    halo_rows,
    near,
    halo_near,
    mine_obs,
    got1,
    part,
    got2,
    total,
    halo_send,
    halo_recv,
    send,
    recv,
    load_sem,
    store_sem,
    row_send,
    row_recv,
):
    lat = lax.axis_index("lat")
    lon = lax.axis_index("lon")
    z = lon // 2
    core = lax.rem(lon, 2)
    mine = lat * 2 + core
    me = lat * N_LON + lon
    north = (lax.rem(lat + 1, N_LAT), lon)
    south = (lax.rem(lat + N_LAT - 1, N_LAT), lon)
    east = (lat, lax.rem(lon + 1, N_LON))
    west = (lat, lax.rem(lon + N_LON - 1, N_LON))
    lane = lax.broadcasted_iota(jnp.int32, (8, 128), 1)
    sub = lax.broadcasted_iota(jnp.int32, (8, 128), 0)

    def other(d):
        return lax.rem(mine + d, GROUP)

    def group_id(n):
        return (n // 2, z * 2 + lax.rem(n, 2))

    def z_step(n):
        return 8 + ((n + 1) // 2) * (2 * lax.rem(n + 1, 2) - 1)

    def z_id(d):
        return (lat, lax.rem(z + d, N_Z) * 2 + core)

    def loop(first, count, body):
        lax.fori_loop(first, count, lambda d, c: (body(d), c)[1], 0)

    load = pltpu.make_async_copy(prior_hbm, prior_ref, load_sem)
    load.start()
    barrier = pltpu.get_barrier_semaphore()

    def greet(peer):
        pl.semaphore_signal(barrier, inc=1, device_id=peer, device_id_type=MESH)

    loop(0, N_Z - 1, lambda n: greet(z_id(z_step(n))))
    loop(1, GROUP, lambda d: greet(group_id(other(d))))
    greet(east)
    greet(west)
    load.wait()

    lanes = lax.broadcasted_iota(jnp.int32, (MEMBERS, 128), 1)

    def edge_plane(p, acc):
        def block(g):
            for i in range(16):
                at = pl.multiple_of(g * 128 + i * 8, 8)
                wide[pl.ds(at, 8), :] = prior_ref[p * MEMBERS + g * 16 + i].astype(F32)
            for r in range(8):
                part_rows = wide[pl.ds(g * 128 + r, 16, stride=8), :]
                rows[p, r, pl.ds(pl.multiple_of(g * 16, 16), 16), :] = part_rows.astype(BF16)

        loop(0, 5, block)
        first, last = acc
        for r in range(8):
            x = rows[p, r].astype(F32)
            here = lanes == p * 8 + r
            first = jnp.where(here, pltpu.roll(x, p * 8 + r, 1), first)
            last = jnp.where(here, pltpu.roll(x, p * 8 + r + 1, 1), last)
        return first, last

    zero = jnp.zeros((MEMBERS, 128), F32)
    first, last = lax.fori_loop(0, PLANES, edge_plane, (zero, zero))
    edge_cols[0] = last.astype(BF16)
    edge_cols[1] = first.astype(BF16)

    halves = []
    for h in range(2):
        owned = jnp.int32(0)
        for n in range(32):
            q = 32 * h + n
            k = order_ref[q // BATCH] * BATCH + q % BATCH
            hit = (tile_ref[k] == me).astype(jnp.int32)
            owned = owned | (hit << n)
        halves.append(owned)

    place = lax.broadcasted_iota(jnp.int32, (NOBS, 128), 0)
    wide_lane = lax.broadcasted_iota(jnp.int32, (NOBS, 128), 1)
    owner = jnp.zeros((NOBS, 128), jnp.int32)
    site = jnp.zeros((NOBS, 128), jnp.int32)
    for q in range(NOBS):
        k = order_ref[q // BATCH] * BATCH + q % BATCH
        owner = jnp.where(place == q, tile_ref[k], owner)
        site = jnp.where(place == q, site_ref[k], site)
    fill = jnp.zeros((128 - MEMBERS, 128), BF16)

    def pick_edge(tile, wanted, r):
        code = jnp.where(owner == tile, site - wanted * 128, -1)
        found = jnp.zeros((NOBS, 128), F32)
        for p in range(PLANES):
            found = found + lax.dot_general(
                (code == wide_lane + p * CELLS).astype(BF16),
                jnp.concatenate([rows[p, r], fill], axis=0),
                (((1,), (1,)), ((), ())),
                preferred_element_type=F32,
            )
        return found.astype(BF16)

    near[0] = pick_edge(me + N_LON, 0, 7)
    near[1] = pick_edge(me - N_LON, 7, 0)

    pl.semaphore_wait(barrier, GROUP - 1 + N_Z - 1 + 2)
    halos = []
    for n, (src, dst, peer) in enumerate(
        (
            (near.at[0], halo_near.at[0], north),
            (near.at[1], halo_near.at[1], south),
            (edge_cols.at[0], halo_cols.at[0], east),
            (edge_cols.at[1], halo_cols.at[1], west),
        )
    ):
        copy = pltpu.make_async_remote_copy(
            src_ref=src,
            dst_ref=dst,
            send_sem=halo_send.at[n],
            recv_sem=halo_recv.at[n],
            device_id=peer,
            device_id_type=MESH,
        )
        copy.start()
        halos.append(copy)
    has_south = (lat > 0).astype(F32)
    has_north = (lat < N_LAT - 1).astype(F32)

    lane1 = lax.broadcasted_iota(jnp.int32, (1, 128), 1)

    def slot(carry):
        lo, hi, table, factors = carry
        use_hi = lo == 0
        word = jnp.where(use_hi, hi, lo)
        low = word & (-word)
        q = jnp.int32(0)
        for bit, pattern in enumerate(
            (-1431655766, -858993460, -252645136, -16711936, -65536)
        ):
            q = q + jnp.where((low & jnp.int32(pattern)) != 0, 1 << bit, 0)
        q = q + jnp.where(use_hi, 32, 0)
        spot = jnp.where(word == 0, NOBS, q)
        lo_next = jnp.where(use_hi, lo, lo & (lo - 1))
        hi_next = jnp.where(use_hi, hi & (hi - 1), hi)
        k = order_ref[q // BATCH] * BATCH + q % BATCH
        s = site_ref[k]
        p = s // CELLS
        r = (s // 128) % 8
        c = s % 128
        around = jnp.concatenate(
            [
                rows[p, r],
                fill,
                rows[p, jnp.maximum(r - 1, 0)],
                fill,
                rows[p, jnp.minimum(r + 1, 7)],
                fill,
            ],
            axis=0,
        )
        shift = jnp.where(sub == 1, -1, jnp.where(sub == 2, 1, 0))
        pick = (lane == c + shift).astype(BF16)
        found = lax.dot_general(
            pick, around, (((1,), (1,)), ((), ())), preferred_element_type=F32
        )
        at_cell = (sub == r) & (lane == c)
        level = p % LEVELS
        cu = jnp.sum(jnp.where(at_cell, wind_ref[level], 0.0), axis=0, keepdims=True)
        cv = jnp.sum(jnp.where(at_cell, wind_ref[LEVELS + level], 0.0), axis=0, keepdims=True)
        cu = jnp.sum(cu, axis=1, keepdims=True)
        cv = jnp.sum(cv, axis=1, keepdims=True)
        x = found[0:1, 0:128]
        xw = found[1:2, 0:128]
        xe = found[2:3, 0:128]
        xs = found[0:1, 128:256] * (r > 0).astype(F32)
        xn = found[0:1, 256:384] * (r < 7).astype(F32)
        cu_up, cu_dn = jnp.maximum(cu, 0.0), jnp.minimum(cu, 0.0)
        cv_up, cv_dn = jnp.maximum(cv, 0.0), jnp.minimum(cv, 0.0)
        f = (
            x
            - cu_up * (x - xw)
            - cu_dn * (xe - x)
            - cv_up * (x - xs)
            - cv_dn * (xn - x)
        )
        four = (
            jnp.where(lane1 == 0, cu_up * (c == 0).astype(F32), 0.0)
            - jnp.where(lane1 == 1, cu_dn * (c == 127).astype(F32), 0.0)
            + jnp.where(lane1 == 2, cv_up * (r == 0).astype(F32), 0.0)
            - jnp.where(lane1 == 3, cv_dn * (r == 7).astype(F32), 0.0)
        )
        factors = jnp.where(place == spot, four, factors)
        table = jnp.where(place == spot, f, table)
        return lo_next, hi_next, table, factors

    def slots(n, carry):
        for _ in range(4):
            carry = slot(carry)
        return carry

    blank = jnp.zeros((NOBS, 128), F32)
    _, _, table, factors = lax.fori_loop(
        0, BATCH // 4, slots, (halves[0], halves[1], blank, blank)
    )
    for copy in halos:
        copy.wait_recv()
    row_of = jnp.bitwise_and(jnp.right_shift(site, 7), 7)
    plane_of = jnp.right_shift(site, 10)
    beside = lax.dot_general(
        (wide_lane == plane_of * 8 + row_of).astype(BF16),
        jnp.concatenate([halo_cols[0], fill, halo_cols[1], fill], axis=0),
        (((1,), (1,)), ((), ())),
        preferred_element_type=F32,
    )
    table = (
        table
        + factors[:, 0:1] * beside[:, 0:128]
        + factors[:, 1:2] * beside[:, 128:256]
        + factors[:, 2:3] * halo_near[0].astype(F32)
        + factors[:, 3:4] * halo_near[1].astype(F32)
    )
    for n in range(GROUP):
        mine_obs[n] = table[2 * n : 2 * n + 2, :]

    def copy1(dst, slot_id):
        return pltpu.make_async_remote_copy(
            src_ref=mine_obs.at[dst],
            dst_ref=got1.at[slot_id],
            send_sem=send.at[0],
            recv_sem=recv.at[0],
            device_id=group_id(dst),
            device_id_type=MESH,
        )

    def copy2(d):
        return pltpu.make_async_remote_copy(
            src_ref=part,
            dst_ref=got2.at[d],
            send_sem=send.at[1],
            recv_sem=recv.at[1],
            device_id=z_id(d),
            device_id_type=MESH,
        )

    def copy3(dst):
        return pltpu.make_async_remote_copy(
            src_ref=total,
            dst_ref=out_ref.at[mine],
            send_sem=send.at[2],
            recv_sem=recv.at[2],
            device_id=group_id(dst),
            device_id_type=MESH,
        )

    def bulk(buffer, count, n):
        return pltpu.make_async_remote_copy(
            src_ref=buffer.at[pl.ds(0, count)],
            dst_ref=buffer.at[pl.ds(0, count)],
            send_sem=send.at[n],
            recv_sem=recv.at[n],
            device_id=north,
            device_id_type=MESH,
        )

    lane16 = lax.broadcasted_iota(jnp.int32, (16, 128), 1)

    def store(p):
        return pltpu.make_async_copy(f_ref.at[p], f_hbm.at[p], store_sem.at[p])

    def forecast(p):
        level = lax.rem(p, LEVELS)
        for r in range(8):
            cu = wind_ref[level, r : r + 1, :]
            cv = wind_ref[LEVELS + level, r : r + 1, :]
            cu_up, cu_dn = jnp.maximum(cu, 0.0), jnp.minimum(cu, 0.0)
            cv_up, cv_dn = jnp.maximum(cv, 0.0), jnp.minimum(cv, 0.0)
            spot = p * 8 + r
            cells = slice(128 * r, 128 * r + 128)
            for g in range(5):
                some = slice(16 * g, 16 * g + 16)
                x = rows[p, r, some, :].astype(F32)
                if r > 0:
                    xs = rows[p, r - 1, some, :].astype(F32)
                else:
                    xs = halo_rows[0, p, some, :].astype(F32) * has_south
                if r < 7:
                    xn = rows[p, r + 1, some, :].astype(F32)
                else:
                    xn = halo_rows[1, p, some, :].astype(F32) * has_north
                from_west = halo_cols[0, some, :].astype(F32)
                from_east = halo_cols[1, some, :].astype(F32)
                xw = jnp.where(
                    lane16 == 0,
                    pltpu.roll(from_west, lax.rem(128 - spot, 128), 1),
                    pltpu.roll(x, 1, 1),
                )
                xe = jnp.where(
                    lane16 == 127, pltpu.roll(from_east, 127 - spot, 1), pltpu.roll(x, 127, 1)
                )
                f = (
                    x
                    - cu_up * (x - xw)
                    - cu_dn * (xe - x)
                    - cv_up * (x - xs)
                    - cv_dn * (xn - x)
                )
                big = f.astype(BF16)
                f_ref[p, some, cells] = big
                low = slice(MEMBERS + 16 * g, MEMBERS + 16 * g + 16)
                f_ref[p, low, cells] = (f - big.astype(F32)).astype(BF16)
        store(p).start()

    def masks():
        word_of = owner // 30
        bit_of = owner - word_of * 30
        own_word = me // 30
        own_bit = jnp.full((8, NOBS), lax.rem(me, 30), jnp.int32)
        chosen = jnp.zeros((NOBS, NOBS), jnp.int32)
        own = jnp.zeros((8, NOBS), jnp.int32)
        for w in range(18):
            word = bits_ref[w : w + 1, :]
            chosen = jnp.where(word_of[:, :NOBS] == w, word, chosen)
            own = jnp.where(jnp.full((8, NOBS), own_word, jnp.int32) == w, word, own)
        scale = 1.0 / (MEMBERS - 1)
        hit = jnp.bitwise_and(jnp.right_shift(chosen, bit_of[:, :NOBS]), 1)
        own_hit = jnp.bitwise_and(jnp.right_shift(own, own_bit), 1)
        mask_ref[:NOBS, :] = hit.astype(F32) * scale
        mask_ref[NOBS:, :] = own_hit.astype(F32) * scale

    loop(1, GROUP, lambda d: copy1(other(d), d).start())
    masks()
    bulk(got1, GROUP - 1, 0).wait_recv()
    acc = mine_obs[mine]
    for d in range(1, GROUP):
        acc = acc + got1[d]
    part[...] = acc
    loop(0, N_Z - 1, lambda n: copy2(z_step(n)).start())
    strips = []
    for n, (src, peer) in enumerate(((rows.at[:, 7], north), (rows.at[:, 0], south))):
        copy = pltpu.make_async_remote_copy(
            src_ref=src,
            dst_ref=halo_rows.at[n],
            send_sem=row_send.at[n],
            recv_sem=row_recv.at[n],
            device_id=peer,
            device_id_type=MESH,
        )
        copy.start()
        strips.append(copy)
    bulk(got2, N_Z - 1, 1).wait_recv()
    acc = part[...]
    for d in range(1, N_Z):
        acc = acc + got2[d]
    total[...] = acc
    loop(1, GROUP, lambda d: copy3(other(d)).start())
    out_ref[mine] = acc
    for copy in strips:
        copy.wait_recv()
    loop(0, PLANES, forecast)
    bulk(out_ref, GROUP - 1, 2).wait_recv()
    for copy in halos + strips:
        copy.wait_send()
    for p in range(PLANES):
        store(p).wait()
    bulk(got1, GROUP - 1, 0).wait_send()
    bulk(got2, N_Z - 1, 1).wait_send()
    bulk(got1, GROUP - 1, 2).wait_send()


def filter_kernel(
    order_ref,
    value_ref,
    var_ref,
    bits_ref,
    obs_ref,
    f_hbm,
    out_hbm,
    table,
    mask_ref,
    own_ref,
    turned,
    f_ref,
    out_ref,
    load_sem,
    store_sem,
):
    load = pltpu.make_async_copy(f_hbm, f_ref, load_sem)
    load.start()
    for n in range(GROUP):
        table[2 * n : 2 * n + 2, :] = obs_ref[n]
    table[NOBS:, :] = jnp.zeros((128 - NOBS, 128), F32)
    state = jnp.transpose(table[...])[:MEMBERS, :]
    table[...] = jnp.zeros((128, 128), F32)
    table[: NOBS + 8, :NOBS] = bits_ref[...]
    masks = jnp.transpose(table[...])[:NOBS, :]
    mask_ref[...] = masks
    own_ref[...] = jnp.broadcast_to(masks[:, NOBS : NOBS + 1], (NOBS, 128))
    means = jnp.sum(state, axis=0, keepdims=True) * (1.0 / MEMBERS)
    anomalies = state - means
    eye = (
        lax.broadcasted_iota(jnp.int32, (MEMBERS, 128), 0)
        == lax.broadcasted_iota(jnp.int32, (MEMBERS, 128), 1)
    ).astype(F32)

    def spread(x, j):
        return jnp.broadcast_to(x[:, j : j + 1], (x.shape[0], 128))

    def total(x):
        return jnp.sum(x, axis=0, keepdims=True)

    def batch(b, carry):
        anomalies, means, turn = carry
        base = order_ref[b] * BATCH
        a = spread(anomalies, 0)
        m = spread(means, 0)
        for j in range(BATCH):
            k = base + j
            r = var_ref[k]
            val = value_ref[k]
            own = own_ref[pl.ds(k, 1), :]
            row = mask_ref[pl.ds(k, 1), :]
            whole = total(a * a) * (1.0 / (MEMBERS - 1)) + (r + EPSILON)
            shrink = 1.0 / (whole + jnp.sqrt(r * whole))
            shift = (val - m) / whole
            if j + 1 < BATCH:
                after = spread(anomalies, j + 1)
                link = total(after * a) * spread(row, j + 1)
                a_next = after - (link * shrink) * a
                m_next = spread(means, j + 1) + link * shift
            cov = total(anomalies * a) * row
            cov_own = total(turn * a) * own
            anomalies = anomalies - (cov * shrink) * a
            means = means + cov * shift
            turn = turn + cov_own * (shift - shrink * a)
            if j + 1 < BATCH:
                a, m = a_next, m_next
        mask_ref[...] = pltpu.roll(mask_ref[...], 128 - BATCH, 1)
        return (
            pltpu.roll(anomalies, 128 - BATCH, 1),
            pltpu.roll(means, 128 - BATCH, 1),
            turn,
        )

    _, _, turn = lax.fori_loop(0, NOBS // BATCH, batch, (anomalies, means, eye))
    high = turn.astype(BF16).astype(F32)
    low = (turn - high)[:, :MEMBERS]
    high = high[:, :MEMBERS]
    left = jnp.concatenate([high, high, low], axis=1).astype(BF16)
    load.wait()

    def store(p):
        block = pl.ds(p * MEMBERS, MEMBERS)
        return pltpu.make_async_copy(out_ref.at[block], out_hbm.at[block], store_sem.at[p])

    def plane(p, _):
        for h in range(4):
            cells = slice(256 * h, 256 * h + 256)
            right = jnp.concatenate([f_ref[p, :, cells], f_ref[p, :MEMBERS, cells]], axis=0)
            result = jnp.dot(left, right, preferred_element_type=F32)
            for i in range(2):
                turned[pl.ds(2 * h + i, MEMBERS, stride=8), :] = result[:, 128 * i : 128 * i + 128]
        out_ref[pl.ds(p * MEMBERS, MEMBERS)] = (
            turned[...].reshape(MEMBERS, 8, 128).astype(BF16)
        )
        store(p).start()
        return 0

    lax.fori_loop(0, PLANES, plane, 0)
    for p in range(PLANES):
        store(p).wait()


def per_device(prior_state, courant, obs_tile, obs_site, obs_value, obs_var, loc_bits, batch_order):
    prior = prior_state.reshape(ROWS, 8, 128)
    wind = courant.reshape(2 * LEVELS, 8, 128)
    dma = pltpu.SemaphoreType.DMA
    forecast, observed, masks = pl.pallas_call(
        exchange_kernel,
        out_shape=(
            jax.ShapeDtypeStruct((PLANES, 2 * MEMBERS, CELLS), BF16),
            jax.ShapeDtypeStruct((GROUP, 2, 128), F32),
            jax.ShapeDtypeStruct((NOBS + 8, NOBS), F32),
        ),
        in_specs=[spec(SM)] * 3 + [spec(pl.ANY)] + [spec(VM)] * 2,
        out_specs=(spec(pl.ANY), spec(VM), spec(VM)),
        scratch_shapes=[
            VM((ROWS, 8, 128), BF16),
            VM((PLANES, 2 * MEMBERS, CELLS), BF16),
            VM((MEMBERS * 8, 128), F32),
            VM((PLANES, 8, MEMBERS, 128), BF16),
            VM((2, MEMBERS, 128), BF16),
            VM((2, MEMBERS, 128), BF16),
            VM((2, PLANES, MEMBERS, 128), BF16),
            VM((2, NOBS, 128), BF16),
            VM((2, NOBS, 128), BF16),
            VM((GROUP, 2, 128), F32),
            VM((GROUP, 2, 128), F32),
            VM((2, 128), F32),
            VM((N_Z, 2, 128), F32),
            VM((2, 128), F32),
            dma((4,)),
            dma((4,)),
            dma((3,)),
            dma((3,)),
            dma,
            dma((PLANES,)),
            dma((2,)),
            dma((2,)),
        ],
        compiler_params=pltpu.CompilerParams(collective_id=0, has_side_effects=True),
        name="exchange",
    )(obs_tile, obs_site, batch_order, prior, wind, loc_bits.T)
    analysis = pl.pallas_call(
        filter_kernel,
        out_shape=jax.ShapeDtypeStruct((ROWS, 8, 128), BF16),
        in_specs=[spec(SM)] * 3 + [spec(VM)] * 2 + [spec(pl.ANY)],
        out_specs=spec(pl.ANY),
        scratch_shapes=[
            VM((128, 128), F32),
            VM((NOBS, 128), F32),
            VM((NOBS, 128), F32),
            VM((MEMBERS * 8, 128), F32),
            VM((PLANES, 2 * MEMBERS, CELLS), BF16),
            VM((ROWS, 8, 128), BF16),
            dma,
            dma((PLANES,)),
        ],
        name="filter",
    )(batch_order, obs_value, obs_var, masks, observed, forecast)
    return analysis.reshape(prior_state.shape)


def solution(mesh):
    placed = (
        P(None, None, None, "lat", "lon"),
        P(None, None, "lat", "lon"),
        P(),
        P(),
        P(),
        P(),
        P(),
        P(),
    )
    return jax.shard_map(
        per_device,
        mesh=mesh,
        in_specs=placed,
        out_specs=P(None, None, None, "lat", "lon"),
        check_vma=False,
    )
```

```python
import jax
import jax.numpy as jnp
from jax import lax
from jax.experimental import pallas as pl
from jax.experimental.pallas import tpu as pltpu
from jax.sharding import PartitionSpec as P

MESH = pl.DeviceIdType.MESH
EPSILON = 1e-05
MEMBERS = 80
PLANES = 8
LEVELS = 4
CELLS = 1024
NOBS = 64
BATCH = 16
N_LAT = 16
N_LON = 32
N_Z = 16
GROUP = 32
ROWS = PLANES * MEMBERS
F32 = jnp.float32
BF16 = jnp.bfloat16
VM = pltpu.VMEM
SM = pltpu.SMEM


def spec(space):
    return pl.BlockSpec(memory_space=space)


def exchange_kernel(
    tile_ref,
    site_ref,
    order_ref,
    prior_hbm,
    wind_ref,
    bits_ref,
    f_hbm,
    out_ref,
    mask_ref,
    prior_ref,
    f_ref,
    wide,
    rows,
    edge_cols,
    halo_cols,
    halo_rows,
    near,
    halo_near,
    mine_obs,
    got1,
    part,
    got2,
    total,
    halo_send,
    halo_recv,
    send,
    recv,
    load_sem,
    store_sem,
    row_send,
    row_recv,
    ready_up,
    ready_down,
):
    lat = lax.axis_index("lat")
    lon = lax.axis_index("lon")
    z = lon // 2
    core = lax.rem(lon, 2)
    mine = lat * 2 + core
    me = lat * N_LON + lon
    north = (lax.rem(lat + 1, N_LAT), lon)
    south = (lax.rem(lat + N_LAT - 1, N_LAT), lon)
    east = (lat, lax.rem(lon + 1, N_LON))
    west = (lat, lax.rem(lon + N_LON - 1, N_LON))
    lane = lax.broadcasted_iota(jnp.int32, (8, 128), 1)
    sub = lax.broadcasted_iota(jnp.int32, (8, 128), 0)

    def other(d):
        return lax.rem(mine + d, GROUP)

    def group_id(n):
        return (n // 2, z * 2 + lax.rem(n, 2))

    def z_step(n):
        return 8 + ((n + 1) // 2) * (2 * lax.rem(n + 1, 2) - 1)

    def z_id(d):
        return (lat, lax.rem(z + d, N_Z) * 2 + core)

    def loop(first, count, body):
        lax.fori_loop(first, count, lambda d, c: (body(d), c)[1], 0)

    load = pltpu.make_async_copy(prior_hbm, prior_ref, load_sem)
    load.start()
    barrier = pltpu.get_barrier_semaphore()

    def greet(peer):
        pl.semaphore_signal(barrier, inc=1, device_id=peer, device_id_type=MESH)

    greet(z_id(1))
    greet(z_id(N_Z - 1))
    loop(1, GROUP, lambda d: greet(group_id(other(d))))
    greet(east)
    greet(west)
    load.wait()

    lanes = lax.broadcasted_iota(jnp.int32, (MEMBERS, 128), 1)

    def edge_plane(p, acc):
        def block(g):
            for i in range(16):
                at = pl.multiple_of(g * 128 + i * 8, 8)
                wide[pl.ds(at, 8), :] = prior_ref[p * MEMBERS + g * 16 + i].astype(F32)
            for r in range(8):
                part_rows = wide[pl.ds(g * 128 + r, 16, stride=8), :]
                rows[p, r, pl.ds(pl.multiple_of(g * 16, 16), 16), :] = part_rows.astype(BF16)

        loop(0, 5, block)
        first, last = acc
        for r in range(8):
            x = rows[p, r].astype(F32)
            here = lanes == p * 8 + r
            first = jnp.where(here, pltpu.roll(x, p * 8 + r, 1), first)
            last = jnp.where(here, pltpu.roll(x, p * 8 + r + 1, 1), last)
        return first, last

    zero = jnp.zeros((MEMBERS, 128), F32)
    first, last = lax.fori_loop(0, PLANES, edge_plane, (zero, zero))
    edge_cols[0] = last.astype(BF16)
    edge_cols[1] = first.astype(BF16)

    halves = []
    for h in range(2):
        owned = jnp.int32(0)
        for n in range(32):
            q = 32 * h + n
            k = order_ref[q // BATCH] * BATCH + q % BATCH
            hit = (tile_ref[k] == me).astype(jnp.int32)
            owned = owned | (hit << n)
        halves.append(owned)

    place = lax.broadcasted_iota(jnp.int32, (NOBS, 128), 0)
    wide_lane = lax.broadcasted_iota(jnp.int32, (NOBS, 128), 1)
    owner = jnp.zeros((NOBS, 128), jnp.int32)
    site = jnp.zeros((NOBS, 128), jnp.int32)
    for q in range(NOBS):
        k = order_ref[q // BATCH] * BATCH + q % BATCH
        owner = jnp.where(place == q, tile_ref[k], owner)
        site = jnp.where(place == q, site_ref[k], site)
    fill = jnp.zeros((128 - MEMBERS, 128), BF16)

    def pick_edge(tile, wanted, r):
        code = jnp.where(owner == tile, site - wanted * 128, -1)
        found = jnp.zeros((NOBS, 128), F32)
        for p in range(PLANES):
            found = found + lax.dot_general(
                (code == wide_lane + p * CELLS).astype(BF16),
                jnp.concatenate([rows[p, r], fill], axis=0),
                (((1,), (1,)), ((), ())),
                preferred_element_type=F32,
            )
        return found.astype(BF16)

    near[0] = pick_edge(me + N_LON, 0, 7)
    near[1] = pick_edge(me - N_LON, 7, 0)

    def tell(step):
        reach = (1, 2, 4)[step]
        pl.semaphore_signal(
            ready_up.at[step], inc=1, device_id=z_id(reach), device_id_type=MESH
        )
        pl.semaphore_signal(
            ready_down.at[step], inc=1, device_id=z_id(N_Z - reach), device_id_type=MESH
        )

    def hear(step):
        pl.semaphore_wait(ready_up.at[step], 1)
        pl.semaphore_wait(ready_down.at[step], 1)

    pl.semaphore_wait(barrier, GROUP - 1 + 2 + 2)
    tell(0)
    halos = []
    for n, (src, dst, peer) in enumerate(
        (
            (near.at[0], halo_near.at[0], north),
            (near.at[1], halo_near.at[1], south),
            (edge_cols.at[0], halo_cols.at[0], east),
            (edge_cols.at[1], halo_cols.at[1], west),
        )
    ):
        copy = pltpu.make_async_remote_copy(
            src_ref=src,
            dst_ref=dst,
            send_sem=halo_send.at[n],
            recv_sem=halo_recv.at[n],
            device_id=peer,
            device_id_type=MESH,
        )
        copy.start()
        halos.append(copy)
    has_south = (lat > 0).astype(F32)
    has_north = (lat < N_LAT - 1).astype(F32)

    lane1 = lax.broadcasted_iota(jnp.int32, (1, 128), 1)

    def slot(carry):
        lo, hi, table, factors = carry
        use_hi = lo == 0
        word = jnp.where(use_hi, hi, lo)
        low = word & (-word)
        q = jnp.int32(0)
        for bit, pattern in enumerate(
            (-1431655766, -858993460, -252645136, -16711936, -65536)
        ):
            q = q + jnp.where((low & jnp.int32(pattern)) != 0, 1 << bit, 0)
        q = q + jnp.where(use_hi, 32, 0)
        spot = jnp.where(word == 0, NOBS, q)
        lo_next = jnp.where(use_hi, lo, lo & (lo - 1))
        hi_next = jnp.where(use_hi, hi & (hi - 1), hi)
        k = order_ref[q // BATCH] * BATCH + q % BATCH
        s = site_ref[k]
        p = s // CELLS
        r = (s // 128) % 8
        c = s % 128
        around = jnp.concatenate(
            [
                rows[p, r],
                fill,
                rows[p, jnp.maximum(r - 1, 0)],
                fill,
                rows[p, jnp.minimum(r + 1, 7)],
                fill,
            ],
            axis=0,
        )
        shift = jnp.where(sub == 1, -1, jnp.where(sub == 2, 1, 0))
        pick = (lane == c + shift).astype(BF16)
        found = lax.dot_general(
            pick, around, (((1,), (1,)), ((), ())), preferred_element_type=F32
        )
        at_cell = (sub == r) & (lane == c)
        level = p % LEVELS
        cu = jnp.sum(jnp.where(at_cell, wind_ref[level], 0.0), axis=0, keepdims=True)
        cv = jnp.sum(jnp.where(at_cell, wind_ref[LEVELS + level], 0.0), axis=0, keepdims=True)
        cu = jnp.sum(cu, axis=1, keepdims=True)
        cv = jnp.sum(cv, axis=1, keepdims=True)
        x = found[0:1, 0:128]
        xw = found[1:2, 0:128]
        xe = found[2:3, 0:128]
        xs = found[0:1, 128:256] * (r > 0).astype(F32)
        xn = found[0:1, 256:384] * (r < 7).astype(F32)
        cu_up, cu_dn = jnp.maximum(cu, 0.0), jnp.minimum(cu, 0.0)
        cv_up, cv_dn = jnp.maximum(cv, 0.0), jnp.minimum(cv, 0.0)
        f = (
            x
            - cu_up * (x - xw)
            - cu_dn * (xe - x)
            - cv_up * (x - xs)
            - cv_dn * (xn - x)
        )
        four = (
            jnp.where(lane1 == 0, cu_up * (c == 0).astype(F32), 0.0)
            - jnp.where(lane1 == 1, cu_dn * (c == 127).astype(F32), 0.0)
            + jnp.where(lane1 == 2, cv_up * (r == 0).astype(F32), 0.0)
            - jnp.where(lane1 == 3, cv_dn * (r == 7).astype(F32), 0.0)
        )
        factors = jnp.where(place == spot, four, factors)
        table = jnp.where(place == spot, f, table)
        return lo_next, hi_next, table, factors

    def slots(n, carry):
        for _ in range(4):
            carry = slot(carry)
        return carry

    blank = jnp.zeros((NOBS, 128), F32)
    state = lax.fori_loop(0, 2, slots, (halves[0], halves[1], blank, blank))
    hear(0)
    tell(1)
    _, _, table, factors = lax.fori_loop(2, BATCH // 4, slots, state)
    for copy in halos:
        copy.wait_recv()
    hear(1)
    tell(2)
    row_of = jnp.bitwise_and(jnp.right_shift(site, 7), 7)
    plane_of = jnp.right_shift(site, 10)
    beside = lax.dot_general(
        (wide_lane == plane_of * 8 + row_of).astype(BF16),
        jnp.concatenate([halo_cols[0], fill, halo_cols[1], fill], axis=0),
        (((1,), (1,)), ((), ())),
        preferred_element_type=F32,
    )
    table = (
        table
        + factors[:, 0:1] * beside[:, 0:128]
        + factors[:, 1:2] * beside[:, 128:256]
        + factors[:, 2:3] * halo_near[0].astype(F32)
        + factors[:, 3:4] * halo_near[1].astype(F32)
    )
    for n in range(GROUP):
        mine_obs[n] = table[2 * n : 2 * n + 2, :]

    def copy1(dst, slot_id):
        return pltpu.make_async_remote_copy(
            src_ref=mine_obs.at[dst],
            dst_ref=got1.at[slot_id],
            send_sem=send.at[0],
            recv_sem=recv.at[0],
            device_id=group_id(dst),
            device_id_type=MESH,
        )

    def copy2(d):
        return pltpu.make_async_remote_copy(
            src_ref=part,
            dst_ref=got2.at[d],
            send_sem=send.at[1],
            recv_sem=recv.at[1],
            device_id=z_id(d),
            device_id_type=MESH,
        )

    def copy3(dst):
        return pltpu.make_async_remote_copy(
            src_ref=total,
            dst_ref=out_ref.at[mine],
            send_sem=send.at[2],
            recv_sem=recv.at[2],
            device_id=group_id(dst),
            device_id_type=MESH,
        )

    def bulk(buffer, count, n):
        return pltpu.make_async_remote_copy(
            src_ref=buffer.at[pl.ds(0, count)],
            dst_ref=buffer.at[pl.ds(0, count)],
            send_sem=send.at[n],
            recv_sem=recv.at[n],
            device_id=north,
            device_id_type=MESH,
        )

    lane16 = lax.broadcasted_iota(jnp.int32, (16, 128), 1)

    def store(p):
        return pltpu.make_async_copy(f_ref.at[p], f_hbm.at[p], store_sem.at[p])

    def forecast(p):
        level = lax.rem(p, LEVELS)
        for r in range(8):
            cu = wind_ref[level, r : r + 1, :]
            cv = wind_ref[LEVELS + level, r : r + 1, :]
            cu_up, cu_dn = jnp.maximum(cu, 0.0), jnp.minimum(cu, 0.0)
            cv_up, cv_dn = jnp.maximum(cv, 0.0), jnp.minimum(cv, 0.0)
            spot = p * 8 + r
            cells = slice(128 * r, 128 * r + 128)
            for g in range(5):
                some = slice(16 * g, 16 * g + 16)
                x = rows[p, r, some, :].astype(F32)
                if r > 0:
                    xs = rows[p, r - 1, some, :].astype(F32)
                else:
                    xs = halo_rows[0, p, some, :].astype(F32) * has_south
                if r < 7:
                    xn = rows[p, r + 1, some, :].astype(F32)
                else:
                    xn = halo_rows[1, p, some, :].astype(F32) * has_north
                from_west = halo_cols[0, some, :].astype(F32)
                from_east = halo_cols[1, some, :].astype(F32)
                xw = jnp.where(
                    lane16 == 0,
                    pltpu.roll(from_west, lax.rem(128 - spot, 128), 1),
                    pltpu.roll(x, 1, 1),
                )
                xe = jnp.where(
                    lane16 == 127, pltpu.roll(from_east, 127 - spot, 1), pltpu.roll(x, 127, 1)
                )
                f = (
                    x
                    - cu_up * (x - xw)
                    - cu_dn * (xe - x)
                    - cv_up * (x - xs)
                    - cv_dn * (xn - x)
                )
                big = f.astype(BF16)
                f_ref[p, some, cells] = big
                low = slice(MEMBERS + 16 * g, MEMBERS + 16 * g + 16)
                f_ref[p, low, cells] = (f - big.astype(F32)).astype(BF16)
        store(p).start()

    def masks():
        word_of = owner // 30
        bit_of = owner - word_of * 30
        own_word = me // 30
        own_bit = jnp.full((8, NOBS), lax.rem(me, 30), jnp.int32)
        chosen = jnp.zeros((NOBS, NOBS), jnp.int32)
        own = jnp.zeros((8, NOBS), jnp.int32)
        for w in range(18):
            word = bits_ref[w : w + 1, :]
            chosen = jnp.where(word_of[:, :NOBS] == w, word, chosen)
            own = jnp.where(jnp.full((8, NOBS), own_word, jnp.int32) == w, word, own)
        scale = 1.0 / (MEMBERS - 1)
        hit = jnp.bitwise_and(jnp.right_shift(chosen, bit_of[:, :NOBS]), 1)
        own_hit = jnp.bitwise_and(jnp.right_shift(own, own_bit), 1)
        mask_ref[:NOBS, :] = hit.astype(F32) * scale
        mask_ref[NOBS:, :] = own_hit.astype(F32) * scale

    loop(1, GROUP, lambda d: copy1(other(d), d).start())
    masks()
    hear(2)
    bulk(got1, GROUP - 1, 0).wait_recv()
    acc = mine_obs[mine]
    for d in range(1, GROUP):
        acc = acc + got1[d]
    part[...] = acc
    loop(0, N_Z - 1, lambda n: copy2(z_step(n)).start())
    strips = []
    for n, (src, peer) in enumerate(((rows.at[:, 7], north), (rows.at[:, 0], south))):
        copy = pltpu.make_async_remote_copy(
            src_ref=src,
            dst_ref=halo_rows.at[n],
            send_sem=row_send.at[n],
            recv_sem=row_recv.at[n],
            device_id=peer,
            device_id_type=MESH,
        )
        copy.start()
        strips.append(copy)
    bulk(got2, N_Z - 1, 1).wait_recv()
    acc = part[...]
    for d in range(1, N_Z):
        acc = acc + got2[d]
    total[...] = acc
    loop(1, GROUP, lambda d: copy3(other(d)).start())
    out_ref[mine] = acc
    for copy in strips:
        copy.wait_recv()
    loop(0, PLANES, forecast)
    bulk(out_ref, GROUP - 1, 2).wait_recv()
    for copy in halos + strips:
        copy.wait_send()
    for p in range(PLANES):
        store(p).wait()
    bulk(got1, GROUP - 1, 0).wait_send()
    bulk(got2, N_Z - 1, 1).wait_send()
    bulk(got1, GROUP - 1, 2).wait_send()


def filter_kernel(
    order_ref,
    value_ref,
    var_ref,
    bits_ref,
    obs_ref,
    f_hbm,
    out_hbm,
    table,
    mask_ref,
    own_ref,
    turned,
    f_ref,
    out_ref,
    load_sem,
    store_sem,
):
    load = pltpu.make_async_copy(f_hbm, f_ref, load_sem)
    load.start()
    for n in range(GROUP):
        table[2 * n : 2 * n + 2, :] = obs_ref[n]
    table[NOBS:, :] = jnp.zeros((128 - NOBS, 128), F32)
    state = jnp.transpose(table[...])[:MEMBERS, :]
    table[...] = jnp.zeros((128, 128), F32)
    table[: NOBS + 8, :NOBS] = bits_ref[...]
    masks = jnp.transpose(table[...])[:NOBS, :]
    mask_ref[...] = masks
    own_ref[...] = jnp.broadcast_to(masks[:, NOBS : NOBS + 1], (NOBS, 128))
    means = jnp.sum(state, axis=0, keepdims=True) * (1.0 / MEMBERS)
    anomalies = state - means
    eye = (
        lax.broadcasted_iota(jnp.int32, (MEMBERS, 128), 0)
        == lax.broadcasted_iota(jnp.int32, (MEMBERS, 128), 1)
    ).astype(F32)

    def spread(x, j):
        return jnp.broadcast_to(x[:, j : j + 1], (x.shape[0], 128))

    def total(x):
        return jnp.sum(x, axis=0, keepdims=True)

    def batch(b, carry):
        anomalies, means, turn = carry
        base = order_ref[b] * BATCH
        a = spread(anomalies, 0)
        m = spread(means, 0)
        for j in range(BATCH):
            k = base + j
            r = var_ref[k]
            val = value_ref[k]
            own = own_ref[pl.ds(k, 1), :]
            row = mask_ref[pl.ds(k, 1), :]
            whole = total(a * a) * (1.0 / (MEMBERS - 1)) + (r + EPSILON)
            shrink = 1.0 / (whole + jnp.sqrt(r * whole))
            shift = (val - m) / whole
            if j + 1 < BATCH:
                after = spread(anomalies, j + 1)
                link = total(after * a) * spread(row, j + 1)
                a_next = after - (link * shrink) * a
                m_next = spread(means, j + 1) + link * shift
            cov = total(anomalies * a) * row
            cov_own = total(turn * a) * own
            anomalies = anomalies - (cov * shrink) * a
            means = means + cov * shift
            turn = turn + cov_own * (shift - shrink * a)
            if j + 1 < BATCH:
                a, m = a_next, m_next
        mask_ref[...] = pltpu.roll(mask_ref[...], 128 - BATCH, 1)
        return (
            pltpu.roll(anomalies, 128 - BATCH, 1),
            pltpu.roll(means, 128 - BATCH, 1),
            turn,
        )

    _, _, turn = lax.fori_loop(0, NOBS // BATCH, batch, (anomalies, means, eye))
    high = turn.astype(BF16).astype(F32)
    low = (turn - high)[:, :MEMBERS]
    high = high[:, :MEMBERS]
    left = jnp.concatenate([high, high, low], axis=1).astype(BF16)
    load.wait()

    def store(p):
        block = pl.ds(p * MEMBERS, MEMBERS)
        return pltpu.make_async_copy(out_ref.at[block], out_hbm.at[block], store_sem.at[p])

    def plane(p, _):
        for h in range(4):
            cells = slice(256 * h, 256 * h + 256)
            right = jnp.concatenate([f_ref[p, :, cells], f_ref[p, :MEMBERS, cells]], axis=0)
            result = jnp.dot(left, right, preferred_element_type=F32)
            for i in range(2):
                turned[pl.ds(2 * h + i, MEMBERS, stride=8), :] = result[:, 128 * i : 128 * i + 128]
        out_ref[pl.ds(p * MEMBERS, MEMBERS)] = (
            turned[...].reshape(MEMBERS, 8, 128).astype(BF16)
        )
        store(p).start()
        return 0

    lax.fori_loop(0, PLANES, plane, 0)
    for p in range(PLANES):
        store(p).wait()


def per_device(prior_state, courant, obs_tile, obs_site, obs_value, obs_var, loc_bits, batch_order):
    prior = prior_state.reshape(ROWS, 8, 128)
    wind = courant.reshape(2 * LEVELS, 8, 128)
    dma = pltpu.SemaphoreType.DMA
    forecast, observed, masks = pl.pallas_call(
        exchange_kernel,
        out_shape=(
            jax.ShapeDtypeStruct((PLANES, 2 * MEMBERS, CELLS), BF16),
            jax.ShapeDtypeStruct((GROUP, 2, 128), F32),
            jax.ShapeDtypeStruct((NOBS + 8, NOBS), F32),
        ),
        in_specs=[spec(SM)] * 3 + [spec(pl.ANY)] + [spec(VM)] * 2,
        out_specs=(spec(pl.ANY), spec(VM), spec(VM)),
        scratch_shapes=[
            VM((ROWS, 8, 128), BF16),
            VM((PLANES, 2 * MEMBERS, CELLS), BF16),
            VM((MEMBERS * 8, 128), F32),
            VM((PLANES, 8, MEMBERS, 128), BF16),
            VM((2, MEMBERS, 128), BF16),
            VM((2, MEMBERS, 128), BF16),
            VM((2, PLANES, MEMBERS, 128), BF16),
            VM((2, NOBS, 128), BF16),
            VM((2, NOBS, 128), BF16),
            VM((GROUP, 2, 128), F32),
            VM((GROUP, 2, 128), F32),
            VM((2, 128), F32),
            VM((N_Z, 2, 128), F32),
            VM((2, 128), F32),
            dma((4,)),
            dma((4,)),
            dma((3,)),
            dma((3,)),
            dma,
            dma((PLANES,)),
            dma((2,)),
            dma((2,)),
            pltpu.SemaphoreType.REGULAR((3,)),
            pltpu.SemaphoreType.REGULAR((3,)),
        ],
        compiler_params=pltpu.CompilerParams(collective_id=0, has_side_effects=True),
        name="exchange",
    )(obs_tile, obs_site, batch_order, prior, wind, loc_bits.T)
    analysis = pl.pallas_call(
        filter_kernel,
        out_shape=jax.ShapeDtypeStruct((ROWS, 8, 128), BF16),
        in_specs=[spec(SM)] * 3 + [spec(VM)] * 2 + [spec(pl.ANY)],
        out_specs=spec(pl.ANY),
        scratch_shapes=[
            VM((128, 128), F32),
            VM((NOBS, 128), F32),
            VM((NOBS, 128), F32),
            VM((MEMBERS * 8, 128), F32),
            VM((PLANES, 2 * MEMBERS, CELLS), BF16),
            VM((ROWS, 8, 128), BF16),
            dma,
            dma((PLANES,)),
        ],
        name="filter",
    )(batch_order, obs_value, obs_var, masks, observed, forecast)
    return analysis.reshape(prior_state.shape)


def solution(mesh):
    placed = (
        P(None, None, None, "lat", "lon"),
        P(None, None, "lat", "lon"),
        P(),
        P(),
        P(),
        P(),
        P(),
        P(),
    )
    return jax.shard_map(
        per_device,
        mesh=mesh,
        in_specs=placed,
        out_specs=P(None, None, None, "lat", "lon"),
        check_vma=False,
    )
```

```python
import jax
import jax.numpy as jnp
from jax import lax
from jax.experimental import pallas as pl
from jax.experimental.pallas import tpu as pltpu
from jax.sharding import PartitionSpec as P

MESH = pl.DeviceIdType.MESH
EPSILON = 1e-05
MEMBERS = 80
PLANES = 8
LEVELS = 4
CELLS = 1024
NOBS = 64
BATCH = 16
N_LAT = 16
N_LON = 32
N_Z = 16
GROUP = 32
ROWS = PLANES * MEMBERS
F32 = jnp.float32
BF16 = jnp.bfloat16
VM = pltpu.VMEM
SM = pltpu.SMEM


def spec(space):
    return pl.BlockSpec(memory_space=space)


def exchange_kernel(
    tile_ref,
    site_ref,
    order_ref,
    prior_hbm,
    wind_ref,
    bits_ref,
    f_hbm,
    out_ref,
    mask_ref,
    prior_ref,
    f_ref,
    wide,
    rows,
    edge_cols,
    halo_cols,
    halo_rows,
    near,
    halo_near,
    mine_obs,
    got1,
    part,
    got2,
    total,
    halo_send,
    halo_recv,
    send,
    recv,
    load_sem,
    store_sem,
    row_send,
    row_recv,
    ready_up,
    ready_down,
):
    lat = lax.axis_index("lat")
    lon = lax.axis_index("lon")
    z = lon // 2
    core = lax.rem(lon, 2)
    mine = lat * 2 + core
    me = lat * N_LON + lon
    north = (lax.rem(lat + 1, N_LAT), lon)
    south = (lax.rem(lat + N_LAT - 1, N_LAT), lon)
    east = (lat, lax.rem(lon + 1, N_LON))
    west = (lat, lax.rem(lon + N_LON - 1, N_LON))
    lane = lax.broadcasted_iota(jnp.int32, (8, 128), 1)
    sub = lax.broadcasted_iota(jnp.int32, (8, 128), 0)

    def other(d):
        return lax.rem(mine + d, GROUP)

    def group_id(n):
        return (n // 2, z * 2 + lax.rem(n, 2))

    def z_step(n):
        return 8 + ((n + 1) // 2) * (2 * lax.rem(n + 1, 2) - 1)

    def far_step(n):
        return 16 + ((n + 1) // 2) * (2 * lax.rem(n + 1, 2) - 1)

    def z_id(d):
        return (lat, lax.rem(z + d, N_Z) * 2 + core)

    def loop(first, count, body):
        lax.fori_loop(first, count, lambda d, c: (body(d), c)[1], 0)

    load = pltpu.make_async_copy(prior_hbm, prior_ref, load_sem)
    load.start()
    barrier = pltpu.get_barrier_semaphore()

    def greet(peer):
        pl.semaphore_signal(barrier, inc=1, device_id=peer, device_id_type=MESH)

    greet(z_id(1))
    greet(z_id(N_Z - 1))
    loop(1, GROUP, lambda d: greet(group_id(other(d))))
    greet(east)
    greet(west)
    load.wait()

    lanes = lax.broadcasted_iota(jnp.int32, (MEMBERS, 128), 1)

    def edge_plane(p, acc):
        def block(g):
            for i in range(16):
                at = pl.multiple_of(g * 128 + i * 8, 8)
                wide[pl.ds(at, 8), :] = prior_ref[p * MEMBERS + g * 16 + i].astype(F32)
            for r in range(8):
                part_rows = wide[pl.ds(g * 128 + r, 16, stride=8), :]
                rows[p, r, pl.ds(pl.multiple_of(g * 16, 16), 16), :] = part_rows.astype(BF16)

        loop(0, 5, block)
        first, last = acc
        for r in range(8):
            x = rows[p, r].astype(F32)
            here = lanes == p * 8 + r
            first = jnp.where(here, pltpu.roll(x, p * 8 + r, 1), first)
            last = jnp.where(here, pltpu.roll(x, p * 8 + r + 1, 1), last)
        return first, last

    zero = jnp.zeros((MEMBERS, 128), F32)
    first, last = lax.fori_loop(0, PLANES, edge_plane, (zero, zero))
    edge_cols[0] = last.astype(BF16)
    edge_cols[1] = first.astype(BF16)

    halves = []
    for h in range(2):
        owned = jnp.int32(0)
        for n in range(32):
            q = 32 * h + n
            k = order_ref[q // BATCH] * BATCH + q % BATCH
            hit = (tile_ref[k] == me).astype(jnp.int32)
            owned = owned | (hit << n)
        halves.append(owned)

    place = lax.broadcasted_iota(jnp.int32, (NOBS, 128), 0)
    wide_lane = lax.broadcasted_iota(jnp.int32, (NOBS, 128), 1)
    owner = jnp.zeros((NOBS, 128), jnp.int32)
    site = jnp.zeros((NOBS, 128), jnp.int32)
    for q in range(NOBS):
        k = order_ref[q // BATCH] * BATCH + q % BATCH
        owner = jnp.where(place == q, tile_ref[k], owner)
        site = jnp.where(place == q, site_ref[k], site)
    fill = jnp.zeros((128 - MEMBERS, 128), BF16)

    def pick_edge(tile, wanted, r):
        code = jnp.where(owner == tile, site - wanted * 128, -1)
        found = jnp.zeros((NOBS, 128), F32)
        for p in range(PLANES):
            found = found + lax.dot_general(
                (code == wide_lane + p * CELLS).astype(BF16),
                jnp.concatenate([rows[p, r], fill], axis=0),
                (((1,), (1,)), ((), ())),
                preferred_element_type=F32,
            )
        return found.astype(BF16)

    near[0] = pick_edge(me + N_LON, 0, 7)
    near[1] = pick_edge(me - N_LON, 7, 0)

    def tell(step):
        reach = (1, 2, 4)[step]
        pl.semaphore_signal(
            ready_up.at[step], inc=1, device_id=z_id(reach), device_id_type=MESH
        )
        pl.semaphore_signal(
            ready_down.at[step], inc=1, device_id=z_id(N_Z - reach), device_id_type=MESH
        )

    def hear(step):
        pl.semaphore_wait(ready_up.at[step], 1)
        pl.semaphore_wait(ready_down.at[step], 1)

    pl.semaphore_wait(barrier, GROUP - 1 + 2 + 2)
    tell(0)
    halos = []
    for n, (src, dst, peer) in enumerate(
        (
            (near.at[0], halo_near.at[0], north),
            (near.at[1], halo_near.at[1], south),
            (edge_cols.at[0], halo_cols.at[0], east),
            (edge_cols.at[1], halo_cols.at[1], west),
        )
    ):
        copy = pltpu.make_async_remote_copy(
            src_ref=src,
            dst_ref=dst,
            send_sem=halo_send.at[n],
            recv_sem=halo_recv.at[n],
            device_id=peer,
            device_id_type=MESH,
        )
        copy.start()
        halos.append(copy)
    has_south = (lat > 0).astype(F32)
    has_north = (lat < N_LAT - 1).astype(F32)

    lane1 = lax.broadcasted_iota(jnp.int32, (1, 128), 1)

    def slot(carry):
        lo, hi, table, factors = carry
        use_hi = lo == 0
        word = jnp.where(use_hi, hi, lo)
        low = word & (-word)
        q = jnp.int32(0)
        for bit, pattern in enumerate(
            (-1431655766, -858993460, -252645136, -16711936, -65536)
        ):
            q = q + jnp.where((low & jnp.int32(pattern)) != 0, 1 << bit, 0)
        q = q + jnp.where(use_hi, 32, 0)
        spot = jnp.where(word == 0, NOBS, q)
        lo_next = jnp.where(use_hi, lo, lo & (lo - 1))
        hi_next = jnp.where(use_hi, hi & (hi - 1), hi)
        k = order_ref[q // BATCH] * BATCH + q % BATCH
        s = site_ref[k]
        p = s // CELLS
        r = (s // 128) % 8
        c = s % 128
        around = jnp.concatenate(
            [
                rows[p, r],
                fill,
                rows[p, jnp.maximum(r - 1, 0)],
                fill,
                rows[p, jnp.minimum(r + 1, 7)],
                fill,
            ],
            axis=0,
        )
        shift = jnp.where(sub == 1, -1, jnp.where(sub == 2, 1, 0))
        pick = (lane == c + shift).astype(BF16)
        found = lax.dot_general(
            pick, around, (((1,), (1,)), ((), ())), preferred_element_type=F32
        )
        at_cell = (sub == r) & (lane == c)
        level = p % LEVELS
        cu = jnp.sum(jnp.where(at_cell, wind_ref[level], 0.0), axis=0, keepdims=True)
        cv = jnp.sum(jnp.where(at_cell, wind_ref[LEVELS + level], 0.0), axis=0, keepdims=True)
        cu = jnp.sum(cu, axis=1, keepdims=True)
        cv = jnp.sum(cv, axis=1, keepdims=True)
        x = found[0:1, 0:128]
        xw = found[1:2, 0:128]
        xe = found[2:3, 0:128]
        xs = found[0:1, 128:256] * (r > 0).astype(F32)
        xn = found[0:1, 256:384] * (r < 7).astype(F32)
        cu_up, cu_dn = jnp.maximum(cu, 0.0), jnp.minimum(cu, 0.0)
        cv_up, cv_dn = jnp.maximum(cv, 0.0), jnp.minimum(cv, 0.0)
        f = (
            x
            - cu_up * (x - xw)
            - cu_dn * (xe - x)
            - cv_up * (x - xs)
            - cv_dn * (xn - x)
        )
        four = (
            jnp.where(lane1 == 0, cu_up * (c == 0).astype(F32), 0.0)
            - jnp.where(lane1 == 1, cu_dn * (c == 127).astype(F32), 0.0)
            + jnp.where(lane1 == 2, cv_up * (r == 0).astype(F32), 0.0)
            - jnp.where(lane1 == 3, cv_dn * (r == 7).astype(F32), 0.0)
        )
        factors = jnp.where(place == spot, four, factors)
        table = jnp.where(place == spot, f, table)
        return lo_next, hi_next, table, factors

    def slots(n, carry):
        for _ in range(4):
            carry = slot(carry)
        return carry

    blank = jnp.zeros((NOBS, 128), F32)
    state = lax.fori_loop(0, 2, slots, (halves[0], halves[1], blank, blank))
    hear(0)
    tell(1)
    _, _, table, factors = lax.fori_loop(2, BATCH // 4, slots, state)
    for copy in halos:
        copy.wait_recv()
    hear(1)
    tell(2)
    row_of = jnp.bitwise_and(jnp.right_shift(site, 7), 7)
    plane_of = jnp.right_shift(site, 10)
    beside = lax.dot_general(
        (wide_lane == plane_of * 8 + row_of).astype(BF16),
        jnp.concatenate([halo_cols[0], fill, halo_cols[1], fill], axis=0),
        (((1,), (1,)), ((), ())),
        preferred_element_type=F32,
    )
    table = (
        table
        + factors[:, 0:1] * beside[:, 0:128]
        + factors[:, 1:2] * beside[:, 128:256]
        + factors[:, 2:3] * halo_near[0].astype(F32)
        + factors[:, 3:4] * halo_near[1].astype(F32)
    )
    for n in range(GROUP):
        mine_obs[n] = table[2 * n : 2 * n + 2, :]

    def copy1(dst, slot_id):
        return pltpu.make_async_remote_copy(
            src_ref=mine_obs.at[dst],
            dst_ref=got1.at[slot_id],
            send_sem=send.at[0],
            recv_sem=recv.at[0],
            device_id=group_id(dst),
            device_id_type=MESH,
        )

    def copy2(d):
        return pltpu.make_async_remote_copy(
            src_ref=part,
            dst_ref=got2.at[d],
            send_sem=send.at[1],
            recv_sem=recv.at[1],
            device_id=z_id(d),
            device_id_type=MESH,
        )

    def copy3(dst):
        return pltpu.make_async_remote_copy(
            src_ref=total,
            dst_ref=out_ref.at[mine],
            send_sem=send.at[2],
            recv_sem=recv.at[2],
            device_id=group_id(dst),
            device_id_type=MESH,
        )

    def bulk(buffer, count, n):
        return pltpu.make_async_remote_copy(
            src_ref=buffer.at[pl.ds(0, count)],
            dst_ref=buffer.at[pl.ds(0, count)],
            send_sem=send.at[n],
            recv_sem=recv.at[n],
            device_id=north,
            device_id_type=MESH,
        )

    lane16 = lax.broadcasted_iota(jnp.int32, (16, 128), 1)

    def store(p):
        return pltpu.make_async_copy(f_ref.at[p], f_hbm.at[p], store_sem.at[p])

    def forecast(p, which):
        level = lax.rem(p, LEVELS)
        for r in which:
            cu = wind_ref[level, r : r + 1, :]
            cv = wind_ref[LEVELS + level, r : r + 1, :]
            cu_up, cu_dn = jnp.maximum(cu, 0.0), jnp.minimum(cu, 0.0)
            cv_up, cv_dn = jnp.maximum(cv, 0.0), jnp.minimum(cv, 0.0)
            spot = p * 8 + r
            cells = slice(128 * r, 128 * r + 128)
            for g in range(5):
                some = slice(16 * g, 16 * g + 16)
                x = rows[p, r, some, :].astype(F32)
                if r > 0:
                    xs = rows[p, r - 1, some, :].astype(F32)
                else:
                    xs = halo_rows[0, p, some, :].astype(F32) * has_south
                if r < 7:
                    xn = rows[p, r + 1, some, :].astype(F32)
                else:
                    xn = halo_rows[1, p, some, :].astype(F32) * has_north
                from_west = halo_cols[0, some, :].astype(F32)
                from_east = halo_cols[1, some, :].astype(F32)
                xw = jnp.where(
                    lane16 == 0,
                    pltpu.roll(from_west, lax.rem(128 - spot, 128), 1),
                    pltpu.roll(x, 1, 1),
                )
                xe = jnp.where(
                    lane16 == 127, pltpu.roll(from_east, 127 - spot, 1), pltpu.roll(x, 127, 1)
                )
                f = (
                    x
                    - cu_up * (x - xw)
                    - cu_dn * (xe - x)
                    - cv_up * (x - xs)
                    - cv_dn * (xn - x)
                )
                big = f.astype(BF16)
                f_ref[p, some, cells] = big
                low = slice(MEMBERS + 16 * g, MEMBERS + 16 * g + 16)
                f_ref[p, low, cells] = (f - big.astype(F32)).astype(BF16)

    def inner(p):
        forecast(p, range(1, 7))

    def outer(p):
        forecast(p, (0, 7))
        store(p).start()

    def masks():
        word_of = owner // 30
        bit_of = owner - word_of * 30
        own_word = me // 30
        own_bit = jnp.full((8, NOBS), lax.rem(me, 30), jnp.int32)
        chosen = jnp.zeros((NOBS, NOBS), jnp.int32)
        own = jnp.zeros((8, NOBS), jnp.int32)
        for w in range(18):
            word = bits_ref[w : w + 1, :]
            chosen = jnp.where(word_of[:, :NOBS] == w, word, chosen)
            own = jnp.where(jnp.full((8, NOBS), own_word, jnp.int32) == w, word, own)
        scale = 1.0 / (MEMBERS - 1)
        hit = jnp.bitwise_and(jnp.right_shift(chosen, bit_of[:, :NOBS]), 1)
        own_hit = jnp.bitwise_and(jnp.right_shift(own, own_bit), 1)
        mask_ref[:NOBS, :] = hit.astype(F32) * scale
        mask_ref[NOBS:, :] = own_hit.astype(F32) * scale

    loop(0, GROUP - 1, lambda n: copy1(other(far_step(n)), far_step(n)).start())
    masks()
    hear(2)
    bulk(got1, GROUP - 1, 0).wait_recv()
    acc = mine_obs[mine]
    for d in range(1, GROUP):
        acc = acc + got1[d]
    part[...] = acc
    loop(0, N_Z - 1, lambda n: copy2(z_step(n)).start())
    strips = []
    for n, (src, peer) in enumerate(((rows.at[:, 7], north), (rows.at[:, 0], south))):
        copy = pltpu.make_async_remote_copy(
            src_ref=src,
            dst_ref=halo_rows.at[n],
            send_sem=row_send.at[n],
            recv_sem=row_recv.at[n],
            device_id=peer,
            device_id_type=MESH,
        )
        copy.start()
        strips.append(copy)
    loop(0, PLANES, inner)
    bulk(got2, N_Z - 1, 1).wait_recv()
    acc = part[...]
    for d in range(1, N_Z):
        acc = acc + got2[d]
    total[...] = acc
    loop(0, GROUP - 1, lambda n: copy3(other(far_step(n))).start())
    out_ref[mine] = acc
    for copy in strips:
        copy.wait_recv()
    loop(0, PLANES, outer)
    bulk(out_ref, GROUP - 1, 2).wait_recv()
    for copy in halos + strips:
        copy.wait_send()
    for p in range(PLANES):
        store(p).wait()
    bulk(got1, GROUP - 1, 0).wait_send()
    bulk(got2, N_Z - 1, 1).wait_send()
    bulk(got1, GROUP - 1, 2).wait_send()


def filter_kernel(
    order_ref,
    value_ref,
    var_ref,
    bits_ref,
    obs_ref,
    f_hbm,
    out_hbm,
    table,
    mask_ref,
    own_ref,
    turned,
    f_ref,
    out_ref,
    load_sem,
    store_sem,
):
    load = pltpu.make_async_copy(f_hbm, f_ref, load_sem)
    load.start()
    for n in range(GROUP):
        table[2 * n : 2 * n + 2, :] = obs_ref[n]
    table[NOBS:, :] = jnp.zeros((128 - NOBS, 128), F32)
    state = jnp.transpose(table[...])[:MEMBERS, :]
    table[...] = jnp.zeros((128, 128), F32)
    table[: NOBS + 8, :NOBS] = bits_ref[...]
    masks = jnp.transpose(table[...])[:NOBS, :]
    mask_ref[...] = masks
    own_ref[...] = jnp.broadcast_to(masks[:, NOBS : NOBS + 1], (NOBS, 128))
    means = jnp.sum(state, axis=0, keepdims=True) * (1.0 / MEMBERS)
    anomalies = state - means
    eye = (
        lax.broadcasted_iota(jnp.int32, (MEMBERS, 128), 0)
        == lax.broadcasted_iota(jnp.int32, (MEMBERS, 128), 1)
    ).astype(F32)

    def spread(x, j):
        return jnp.broadcast_to(x[:, j : j + 1], (x.shape[0], 128))

    def total(x):
        return jnp.sum(x, axis=0, keepdims=True)

    def batch(b, carry):
        anomalies, means, turn = carry
        base = order_ref[b] * BATCH
        a = spread(anomalies, 0)
        m = spread(means, 0)
        for j in range(BATCH):
            k = base + j
            r = var_ref[k]
            val = value_ref[k]
            own = own_ref[pl.ds(k, 1), :]
            row = mask_ref[pl.ds(k, 1), :]
            whole = total(a * a) * (1.0 / (MEMBERS - 1)) + (r + EPSILON)
            shrink = 1.0 / (whole + jnp.sqrt(r * whole))
            shift = (val - m) / whole
            if j + 1 < BATCH:
                after = spread(anomalies, j + 1)
                link = total(after * a) * spread(row, j + 1)
                a_next = after - (link * shrink) * a
                m_next = spread(means, j + 1) + link * shift
            cov = total(anomalies * a) * row
            cov_own = total(turn * a) * own
            anomalies = anomalies - (cov * shrink) * a
            means = means + cov * shift
            turn = turn + cov_own * (shift - shrink * a)
            if j + 1 < BATCH:
                a, m = a_next, m_next
        mask_ref[...] = pltpu.roll(mask_ref[...], 128 - BATCH, 1)
        return (
            pltpu.roll(anomalies, 128 - BATCH, 1),
            pltpu.roll(means, 128 - BATCH, 1),
            turn,
        )

    _, _, turn = lax.fori_loop(0, NOBS // BATCH, batch, (anomalies, means, eye))
    high = turn.astype(BF16).astype(F32)
    low = (turn - high)[:, :MEMBERS]
    high = high[:, :MEMBERS]
    left = jnp.concatenate([high, high, low], axis=1).astype(BF16)
    load.wait()

    def store(p):
        block = pl.ds(p * MEMBERS, MEMBERS)
        return pltpu.make_async_copy(out_ref.at[block], out_hbm.at[block], store_sem.at[p])

    def plane(p, _):
        for h in range(4):
            cells = slice(256 * h, 256 * h + 256)
            right = jnp.concatenate([f_ref[p, :, cells], f_ref[p, :MEMBERS, cells]], axis=0)
            result = jnp.dot(left, right, preferred_element_type=F32)
            for i in range(2):
                turned[pl.ds(2 * h + i, MEMBERS, stride=8), :] = result[:, 128 * i : 128 * i + 128]
        out_ref[pl.ds(p * MEMBERS, MEMBERS)] = (
            turned[...].reshape(MEMBERS, 8, 128).astype(BF16)
        )
        store(p).start()
        return 0

    lax.fori_loop(0, PLANES, plane, 0)
    for p in range(PLANES):
        store(p).wait()


def per_device(prior_state, courant, obs_tile, obs_site, obs_value, obs_var, loc_bits, batch_order):
    prior = prior_state.reshape(ROWS, 8, 128)
    wind = courant.reshape(2 * LEVELS, 8, 128)
    dma = pltpu.SemaphoreType.DMA
    forecast, observed, masks = pl.pallas_call(
        exchange_kernel,
        out_shape=(
            jax.ShapeDtypeStruct((PLANES, 2 * MEMBERS, CELLS), BF16),
            jax.ShapeDtypeStruct((GROUP, 2, 128), F32),
            jax.ShapeDtypeStruct((NOBS + 8, NOBS), F32),
        ),
        in_specs=[spec(SM)] * 3 + [spec(pl.ANY)] + [spec(VM)] * 2,
        out_specs=(spec(pl.ANY), spec(VM), spec(VM)),
        scratch_shapes=[
            VM((ROWS, 8, 128), BF16),
            VM((PLANES, 2 * MEMBERS, CELLS), BF16),
            VM((MEMBERS * 8, 128), F32),
            VM((PLANES, 8, MEMBERS, 128), BF16),
            VM((2, MEMBERS, 128), BF16),
            VM((2, MEMBERS, 128), BF16),
            VM((2, PLANES, MEMBERS, 128), BF16),
            VM((2, NOBS, 128), BF16),
            VM((2, NOBS, 128), BF16),
            VM((GROUP, 2, 128), F32),
            VM((GROUP, 2, 128), F32),
            VM((2, 128), F32),
            VM((N_Z, 2, 128), F32),
            VM((2, 128), F32),
            dma((4,)),
            dma((4,)),
            dma((3,)),
            dma((3,)),
            dma,
            dma((PLANES,)),
            dma((2,)),
            dma((2,)),
            pltpu.SemaphoreType.REGULAR((3,)),
            pltpu.SemaphoreType.REGULAR((3,)),
        ],
        compiler_params=pltpu.CompilerParams(collective_id=0, has_side_effects=True),
        name="exchange",
    )(obs_tile, obs_site, batch_order, prior, wind, loc_bits.T)
    analysis = pl.pallas_call(
        filter_kernel,
        out_shape=jax.ShapeDtypeStruct((ROWS, 8, 128), BF16),
        in_specs=[spec(SM)] * 3 + [spec(VM)] * 2 + [spec(pl.ANY)],
        out_specs=spec(pl.ANY),
        scratch_shapes=[
            VM((128, 128), F32),
            VM((NOBS, 128), F32),
            VM((NOBS, 128), F32),
            VM((MEMBERS * 8, 128), F32),
            VM((PLANES, 2 * MEMBERS, CELLS), BF16),
            VM((ROWS, 8, 128), BF16),
            dma,
            dma((PLANES,)),
        ],
        name="filter",
    )(batch_order, obs_value, obs_var, masks, observed, forecast)
    return analysis.reshape(prior_state.shape)


def solution(mesh):
    placed = (
        P(None, None, None, "lat", "lon"),
        P(None, None, "lat", "lon"),
        P(),
        P(),
        P(),
        P(),
        P(),
        P(),
    )
    return jax.shard_map(
        per_device,
        mesh=mesh,
        in_specs=placed,
        out_specs=P(None, None, None, "lat", "lon"),
        check_vma=False,
    )
```

```python
import jax
import jax.numpy as jnp
from jax import lax
from jax.experimental import pallas as pl
from jax.experimental.pallas import tpu as pltpu
from jax.sharding import PartitionSpec as P

MESH = pl.DeviceIdType.MESH
EPSILON = 1e-05
MEMBERS = 80
PLANES = 8
LEVELS = 4
CELLS = 1024
NOBS = 64
BATCH = 16
N_LAT = 16
N_LON = 32
N_Z = 16
GROUP = 32
ROWS = PLANES * MEMBERS
F32 = jnp.float32
BF16 = jnp.bfloat16
VM = pltpu.VMEM
SM = pltpu.SMEM


def spec(space):
    return pl.BlockSpec(memory_space=space)


def exchange_kernel(
    tile_ref,
    site_ref,
    order_ref,
    prior_hbm,
    wind_ref,
    bits_ref,
    f_hbm,
    out_ref,
    mask_ref,
    prior_ref,
    f_ref,
    wide,
    rows,
    edge_cols,
    halo_cols,
    halo_rows,
    near,
    halo_near,
    mine_obs,
    got1,
    part,
    got2,
    total,
    halo_send,
    halo_recv,
    send,
    recv,
    load_sem,
    store_sem,
    row_send,
    row_recv,
    ready_up,
    ready_down,
):
    lat = lax.axis_index("lat")
    lon = lax.axis_index("lon")
    z = lon // 2
    core = lax.rem(lon, 2)
    mine = lat * 2 + core
    me = lat * N_LON + lon
    north = (lax.rem(lat + 1, N_LAT), lon)
    south = (lax.rem(lat + N_LAT - 1, N_LAT), lon)
    east = (lat, lax.rem(lon + 1, N_LON))
    west = (lat, lax.rem(lon + N_LON - 1, N_LON))
    lane = lax.broadcasted_iota(jnp.int32, (8, 128), 1)
    sub = lax.broadcasted_iota(jnp.int32, (8, 128), 0)

    def other(d):
        return lax.rem(mine + d, GROUP)

    def group_id(n):
        return (n // 2, z * 2 + lax.rem(n, 2))

    def z_step(n):
        return 8 + ((n + 1) // 2) * (2 * lax.rem(n + 1, 2) - 1)

    def z_id(d):
        return (lat, lax.rem(z + d, N_Z) * 2 + core)

    def loop(first, count, body):
        lax.fori_loop(first, count, lambda d, c: (body(d), c)[1], 0)

    load = pltpu.make_async_copy(prior_hbm, prior_ref, load_sem)
    load.start()
    barrier = pltpu.get_barrier_semaphore()

    def greet(peer):
        pl.semaphore_signal(barrier, inc=1, device_id=peer, device_id_type=MESH)

    greet(z_id(1))
    greet(z_id(N_Z - 1))
    loop(1, GROUP, lambda d: greet(group_id(other(d))))
    greet(east)
    greet(west)
    load.wait()

    lanes = lax.broadcasted_iota(jnp.int32, (MEMBERS, 128), 1)

    def edge_plane(p, acc):
        def block(g):
            for i in range(16):
                at = pl.multiple_of(g * 128 + i * 8, 8)
                wide[pl.ds(at, 8), :] = prior_ref[p * MEMBERS + g * 16 + i].astype(F32)
            for r in range(8):
                part_rows = wide[pl.ds(g * 128 + r, 16, stride=8), :]
                rows[p, r, pl.ds(pl.multiple_of(g * 16, 16), 16), :] = part_rows.astype(BF16)

        loop(0, 5, block)
        first, last = acc
        for r in range(8):
            x = rows[p, r].astype(F32)
            here = lanes == p * 8 + r
            first = jnp.where(here, pltpu.roll(x, p * 8 + r, 1), first)
            last = jnp.where(here, pltpu.roll(x, p * 8 + r + 1, 1), last)
        return first, last

    zero = jnp.zeros((MEMBERS, 128), F32)
    first, last = lax.fori_loop(0, PLANES, edge_plane, (zero, zero))
    edge_cols[0] = last.astype(BF16)
    edge_cols[1] = first.astype(BF16)

    halves = []
    for h in range(2):
        owned = jnp.int32(0)
        for n in range(32):
            q = 32 * h + n
            k = order_ref[q // BATCH] * BATCH + q % BATCH
            hit = (tile_ref[k] == me).astype(jnp.int32)
            owned = owned | (hit << n)
        halves.append(owned)

    place = lax.broadcasted_iota(jnp.int32, (NOBS, 128), 0)
    wide_lane = lax.broadcasted_iota(jnp.int32, (NOBS, 128), 1)
    owner = jnp.zeros((NOBS, 128), jnp.int32)
    site = jnp.zeros((NOBS, 128), jnp.int32)
    for q in range(NOBS):
        k = order_ref[q // BATCH] * BATCH + q % BATCH
        owner = jnp.where(place == q, tile_ref[k], owner)
        site = jnp.where(place == q, site_ref[k], site)
    fill = jnp.zeros((128 - MEMBERS, 128), BF16)

    def pick_edge(tile, wanted, r):
        code = jnp.where(owner == tile, site - wanted * 128, -1)
        found = jnp.zeros((NOBS, 128), F32)
        for p in range(PLANES):
            found = found + lax.dot_general(
                (code == wide_lane + p * CELLS).astype(BF16),
                jnp.concatenate([rows[p, r], fill], axis=0),
                (((1,), (1,)), ((), ())),
                preferred_element_type=F32,
            )
        return found.astype(BF16)

    near[0] = pick_edge(me + N_LON, 0, 7)
    near[1] = pick_edge(me - N_LON, 7, 0)

    def tell(step):
        reach = (1, 2, 4)[step]
        pl.semaphore_signal(
            ready_up.at[step], inc=1, device_id=z_id(reach), device_id_type=MESH
        )
        pl.semaphore_signal(
            ready_down.at[step], inc=1, device_id=z_id(N_Z - reach), device_id_type=MESH
        )

    def hear(step):
        pl.semaphore_wait(ready_up.at[step], 1)
        pl.semaphore_wait(ready_down.at[step], 1)

    pl.semaphore_wait(barrier, GROUP - 1 + 2 + 2)
    tell(0)
    halos = []
    for n, (src, dst, peer) in enumerate(
        (
            (near.at[0], halo_near.at[0], north),
            (near.at[1], halo_near.at[1], south),
            (edge_cols.at[0], halo_cols.at[0], east),
            (edge_cols.at[1], halo_cols.at[1], west),
        )
    ):
        copy = pltpu.make_async_remote_copy(
            src_ref=src,
            dst_ref=dst,
            send_sem=halo_send.at[n],
            recv_sem=halo_recv.at[n],
            device_id=peer,
            device_id_type=MESH,
        )
        copy.start()
        halos.append(copy)
    has_south = (lat > 0).astype(F32)
    has_north = (lat < N_LAT - 1).astype(F32)

    lane1 = lax.broadcasted_iota(jnp.int32, (1, 128), 1)

    def slot(carry):
        lo, hi, table, factors = carry
        use_hi = lo == 0
        word = jnp.where(use_hi, hi, lo)
        low = word & (-word)
        q = jnp.int32(0)
        for bit, pattern in enumerate(
            (-1431655766, -858993460, -252645136, -16711936, -65536)
        ):
            q = q + jnp.where((low & jnp.int32(pattern)) != 0, 1 << bit, 0)
        q = q + jnp.where(use_hi, 32, 0)
        spot = jnp.where(word == 0, NOBS, q)
        lo_next = jnp.where(use_hi, lo, lo & (lo - 1))
        hi_next = jnp.where(use_hi, hi & (hi - 1), hi)
        k = order_ref[q // BATCH] * BATCH + q % BATCH
        s = site_ref[k]
        p = s // CELLS
        r = (s // 128) % 8
        c = s % 128
        around = jnp.concatenate(
            [
                rows[p, r],
                fill,
                rows[p, jnp.maximum(r - 1, 0)],
                fill,
                rows[p, jnp.minimum(r + 1, 7)],
                fill,
            ],
            axis=0,
        )
        shift = jnp.where(sub == 1, -1, jnp.where(sub == 2, 1, 0))
        pick = (lane == c + shift).astype(BF16)
        found = lax.dot_general(
            pick, around, (((1,), (1,)), ((), ())), preferred_element_type=F32
        )
        at_cell = (sub == r) & (lane == c)
        level = p % LEVELS
        cu = jnp.sum(jnp.where(at_cell, wind_ref[level], 0.0), axis=0, keepdims=True)
        cv = jnp.sum(jnp.where(at_cell, wind_ref[LEVELS + level], 0.0), axis=0, keepdims=True)
        cu = jnp.sum(cu, axis=1, keepdims=True)
        cv = jnp.sum(cv, axis=1, keepdims=True)
        x = found[0:1, 0:128]
        xw = found[1:2, 0:128]
        xe = found[2:3, 0:128]
        xs = found[0:1, 128:256] * (r > 0).astype(F32)
        xn = found[0:1, 256:384] * (r < 7).astype(F32)
        cu_up, cu_dn = jnp.maximum(cu, 0.0), jnp.minimum(cu, 0.0)
        cv_up, cv_dn = jnp.maximum(cv, 0.0), jnp.minimum(cv, 0.0)
        f = (
            x
            - cu_up * (x - xw)
            - cu_dn * (xe - x)
            - cv_up * (x - xs)
            - cv_dn * (xn - x)
        )
        four = (
            jnp.where(lane1 == 0, cu_up * (c == 0).astype(F32), 0.0)
            - jnp.where(lane1 == 1, cu_dn * (c == 127).astype(F32), 0.0)
            + jnp.where(lane1 == 2, cv_up * (r == 0).astype(F32), 0.0)
            - jnp.where(lane1 == 3, cv_dn * (r == 7).astype(F32), 0.0)
        )
        factors = jnp.where(place == spot, four, factors)
        table = jnp.where(place == spot, f, table)
        return lo_next, hi_next, table, factors

    def slots(n, carry):
        for _ in range(4):
            carry = slot(carry)
        return carry

    blank = jnp.zeros((NOBS, 128), F32)
    state = lax.fori_loop(0, 2, slots, (halves[0], halves[1], blank, blank))
    hear(0)
    tell(1)
    _, _, table, factors = lax.fori_loop(2, BATCH // 4, slots, state)
    for copy in halos:
        copy.wait_recv()
    hear(1)
    tell(2)
    row_of = jnp.bitwise_and(jnp.right_shift(site, 7), 7)
    plane_of = jnp.right_shift(site, 10)
    beside = lax.dot_general(
        (wide_lane == plane_of * 8 + row_of).astype(BF16),
        jnp.concatenate([halo_cols[0], fill, halo_cols[1], fill], axis=0),
        (((1,), (1,)), ((), ())),
        preferred_element_type=F32,
    )
    table = (
        table
        + factors[:, 0:1] * beside[:, 0:128]
        + factors[:, 1:2] * beside[:, 128:256]
        + factors[:, 2:3] * halo_near[0].astype(F32)
        + factors[:, 3:4] * halo_near[1].astype(F32)
    )
    for n in range(GROUP):
        mine_obs[n] = table[2 * n : 2 * n + 2, :]

    def copy1(dst, slot_id):
        return pltpu.make_async_remote_copy(
            src_ref=mine_obs.at[dst],
            dst_ref=got1.at[slot_id],
            send_sem=send.at[0],
            recv_sem=recv.at[0],
            device_id=group_id(dst),
            device_id_type=MESH,
        )

    def copy2(d):
        return pltpu.make_async_remote_copy(
            src_ref=part,
            dst_ref=got2.at[d],
            send_sem=send.at[1],
            recv_sem=recv.at[1],
            device_id=z_id(d),
            device_id_type=MESH,
        )

    def copy3(dst):
        return pltpu.make_async_remote_copy(
            src_ref=total,
            dst_ref=out_ref.at[mine],
            send_sem=send.at[2],
            recv_sem=recv.at[2],
            device_id=group_id(dst),
            device_id_type=MESH,
        )

    def bulk(buffer, count, n):
        return pltpu.make_async_remote_copy(
            src_ref=buffer.at[pl.ds(0, count)],
            dst_ref=buffer.at[pl.ds(0, count)],
            send_sem=send.at[n],
            recv_sem=recv.at[n],
            device_id=north,
            device_id_type=MESH,
        )

    lane16 = lax.broadcasted_iota(jnp.int32, (16, 128), 1)

    def store(p):
        return pltpu.make_async_copy(f_ref.at[p], f_hbm.at[p], store_sem.at[p])

    def forecast(p, which):
        level = lax.rem(p, LEVELS)
        for r in which:
            cu = wind_ref[level, r : r + 1, :]
            cv = wind_ref[LEVELS + level, r : r + 1, :]
            cu_up, cu_dn = jnp.maximum(cu, 0.0), jnp.minimum(cu, 0.0)
            cv_up, cv_dn = jnp.maximum(cv, 0.0), jnp.minimum(cv, 0.0)
            spot = p * 8 + r
            cells = slice(128 * r, 128 * r + 128)
            for g in range(5):
                some = slice(16 * g, 16 * g + 16)
                x = rows[p, r, some, :].astype(F32)
                if r > 0:
                    xs = rows[p, r - 1, some, :].astype(F32)
                else:
                    xs = halo_rows[0, p, some, :].astype(F32) * has_south
                if r < 7:
                    xn = rows[p, r + 1, some, :].astype(F32)
                else:
                    xn = halo_rows[1, p, some, :].astype(F32) * has_north
                from_west = halo_cols[0, some, :].astype(F32)
                from_east = halo_cols[1, some, :].astype(F32)
                xw = jnp.where(
                    lane16 == 0,
                    pltpu.roll(from_west, lax.rem(128 - spot, 128), 1),
                    pltpu.roll(x, 1, 1),
                )
                xe = jnp.where(
                    lane16 == 127, pltpu.roll(from_east, 127 - spot, 1), pltpu.roll(x, 127, 1)
                )
                f = (
                    x
                    - cu_up * (x - xw)
                    - cu_dn * (xe - x)
                    - cv_up * (x - xs)
                    - cv_dn * (xn - x)
                )
                big = f.astype(BF16)
                f_ref[p, some, cells] = big
                low = slice(MEMBERS + 16 * g, MEMBERS + 16 * g + 16)
                f_ref[p, low, cells] = (f - big.astype(F32)).astype(BF16)

    def inner(p):
        forecast(p, range(1, 7))

    def outer(p):
        forecast(p, (0, 7))
        store(p).start()

    def masks():
        word_of = owner // 30
        bit_of = owner - word_of * 30
        own_word = me // 30
        own_bit = jnp.full((8, NOBS), lax.rem(me, 30), jnp.int32)
        chosen = jnp.zeros((NOBS, NOBS), jnp.int32)
        own = jnp.zeros((8, NOBS), jnp.int32)
        for w in range(18):
            word = bits_ref[w : w + 1, :]
            chosen = jnp.where(word_of[:, :NOBS] == w, word, chosen)
            own = jnp.where(jnp.full((8, NOBS), own_word, jnp.int32) == w, word, own)
        scale = 1.0 / (MEMBERS - 1)
        hit = jnp.bitwise_and(jnp.right_shift(chosen, bit_of[:, :NOBS]), 1)
        own_hit = jnp.bitwise_and(jnp.right_shift(own, own_bit), 1)
        mask_ref[:NOBS, :] = hit.astype(F32) * scale
        mask_ref[NOBS:, :] = own_hit.astype(F32) * scale

    loop(1, GROUP, lambda d: copy1(other(d), d).start())
    masks()
    hear(2)
    bulk(got1, GROUP - 1, 0).wait_recv()
    acc = mine_obs[mine]
    for d in range(1, GROUP):
        acc = acc + got1[d]
    part[...] = acc
    loop(0, N_Z - 1, lambda n: copy2(z_step(n)).start())
    strips = []
    for n, (src, peer) in enumerate(((rows.at[:, 7], north), (rows.at[:, 0], south))):
        copy = pltpu.make_async_remote_copy(
            src_ref=src,
            dst_ref=halo_rows.at[n],
            send_sem=row_send.at[n],
            recv_sem=row_recv.at[n],
            device_id=peer,
            device_id_type=MESH,
        )
        copy.start()
        strips.append(copy)
    loop(0, PLANES, inner)
    bulk(got2, N_Z - 1, 1).wait_recv()
    acc = part[...]
    for d in range(1, N_Z):
        acc = acc + got2[d]
    total[...] = acc
    loop(1, GROUP, lambda d: copy3(other(d)).start())
    out_ref[mine] = acc
    for copy in strips:
        copy.wait_recv()
    loop(0, PLANES, outer)
    bulk(out_ref, GROUP - 1, 2).wait_recv()
    for copy in halos + strips:
        copy.wait_send()
    for p in range(PLANES):
        store(p).wait()
    bulk(got1, GROUP - 1, 0).wait_send()
    bulk(got2, N_Z - 1, 1).wait_send()
    bulk(got1, GROUP - 1, 2).wait_send()


def filter_kernel(
    order_ref,
    value_ref,
    var_ref,
    bits_ref,
    obs_ref,
    f_hbm,
    out_hbm,
    table,
    mask_ref,
    own_ref,
    turned,
    f_ref,
    out_ref,
    load_sem,
    store_sem,
):
    load = pltpu.make_async_copy(f_hbm, f_ref, load_sem)
    load.start()
    for n in range(GROUP):
        table[2 * n : 2 * n + 2, :] = obs_ref[n]
    table[NOBS:, :] = jnp.zeros((128 - NOBS, 128), F32)
    state = jnp.transpose(table[...])[:MEMBERS, :]
    table[...] = jnp.zeros((128, 128), F32)
    table[: NOBS + 8, :NOBS] = bits_ref[...]
    masks = jnp.transpose(table[...])[:NOBS, :]
    mask_ref[...] = masks
    own_ref[...] = jnp.broadcast_to(masks[:, NOBS : NOBS + 1], (NOBS, 128))
    means = jnp.sum(state, axis=0, keepdims=True) * (1.0 / MEMBERS)
    anomalies = state - means
    eye = (
        lax.broadcasted_iota(jnp.int32, (MEMBERS, 128), 0)
        == lax.broadcasted_iota(jnp.int32, (MEMBERS, 128), 1)
    ).astype(F32)

    def spread(x, j):
        return jnp.broadcast_to(x[:, j : j + 1], (x.shape[0], 128))

    def total(x):
        half = x[:40] + x[40:]
        quarter = half[:16] + half[16:32]
        return jnp.sum(quarter[:8] + quarter[8:] + half[32:], axis=0, keepdims=True)

    def batch(b, carry):
        anomalies, means, turn = carry
        base = order_ref[b] * BATCH
        a = spread(anomalies, 0)
        m = spread(means, 0)
        for j in range(BATCH):
            k = base + j
            r = var_ref[k]
            val = value_ref[k]
            own = own_ref[pl.ds(k, 1), :]
            row = mask_ref[pl.ds(k, 1), :]
            whole = total(a * a) * (1.0 / (MEMBERS - 1)) + (r + EPSILON)
            shrink = 1.0 / (whole + jnp.sqrt(r * whole))
            shift = (val - m) / whole
            if j + 1 < BATCH:
                after = spread(anomalies, j + 1)
                link = total(after * a) * spread(row, j + 1)
                a_next = after - (link * shrink) * a
                m_next = spread(means, j + 1) + link * shift
            cov = total(anomalies * a) * row
            cov_own = total(turn * a) * own
            anomalies = anomalies - (cov * shrink) * a
            means = means + cov * shift
            turn = turn + cov_own * (shift - shrink * a)
            if j + 1 < BATCH:
                a, m = a_next, m_next
        mask_ref[...] = pltpu.roll(mask_ref[...], 128 - BATCH, 1)
        return (
            pltpu.roll(anomalies, 128 - BATCH, 1),
            pltpu.roll(means, 128 - BATCH, 1),
            turn,
        )

    _, _, turn = lax.fori_loop(0, NOBS // BATCH, batch, (anomalies, means, eye))
    high = turn.astype(BF16).astype(F32)
    low = (turn - high)[:, :MEMBERS]
    high = high[:, :MEMBERS]
    left = jnp.concatenate([high, high, low], axis=1).astype(BF16)
    load.wait()

    def store(p):
        block = pl.ds(p * MEMBERS, MEMBERS)
        return pltpu.make_async_copy(out_ref.at[block], out_hbm.at[block], store_sem.at[p])

    def plane(p, _):
        for h in range(4):
            cells = slice(256 * h, 256 * h + 256)
            right = jnp.concatenate([f_ref[p, :, cells], f_ref[p, :MEMBERS, cells]], axis=0)
            result = jnp.dot(left, right, preferred_element_type=F32)
            for i in range(2):
                turned[pl.ds(2 * h + i, MEMBERS, stride=8), :] = result[:, 128 * i : 128 * i + 128]
        out_ref[pl.ds(p * MEMBERS, MEMBERS)] = (
            turned[...].reshape(MEMBERS, 8, 128).astype(BF16)
        )
        store(p).start()
        return 0

    lax.fori_loop(0, PLANES, plane, 0)
    for p in range(PLANES):
        store(p).wait()


def per_device(prior_state, courant, obs_tile, obs_site, obs_value, obs_var, loc_bits, batch_order):
    prior = prior_state.reshape(ROWS, 8, 128)
    wind = courant.reshape(2 * LEVELS, 8, 128)
    dma = pltpu.SemaphoreType.DMA
    forecast, observed, masks = pl.pallas_call(
        exchange_kernel,
        out_shape=(
            jax.ShapeDtypeStruct((PLANES, 2 * MEMBERS, CELLS), BF16),
            jax.ShapeDtypeStruct((GROUP, 2, 128), F32),
            jax.ShapeDtypeStruct((NOBS + 8, NOBS), F32),
        ),
        in_specs=[spec(SM)] * 3 + [spec(pl.ANY)] + [spec(VM)] * 2,
        out_specs=(spec(pl.ANY), spec(VM), spec(VM)),
        scratch_shapes=[
            VM((ROWS, 8, 128), BF16),
            VM((PLANES, 2 * MEMBERS, CELLS), BF16),
            VM((MEMBERS * 8, 128), F32),
            VM((PLANES, 8, MEMBERS, 128), BF16),
            VM((2, MEMBERS, 128), BF16),
            VM((2, MEMBERS, 128), BF16),
            VM((2, PLANES, MEMBERS, 128), BF16),
            VM((2, NOBS, 128), BF16),
            VM((2, NOBS, 128), BF16),
            VM((GROUP, 2, 128), F32),
            VM((GROUP, 2, 128), F32),
            VM((2, 128), F32),
            VM((N_Z, 2, 128), F32),
            VM((2, 128), F32),
            dma((4,)),
            dma((4,)),
            dma((3,)),
            dma((3,)),
            dma,
            dma((PLANES,)),
            dma((2,)),
            dma((2,)),
            pltpu.SemaphoreType.REGULAR((3,)),
            pltpu.SemaphoreType.REGULAR((3,)),
        ],
        compiler_params=pltpu.CompilerParams(collective_id=0, has_side_effects=True),
        name="exchange",
    )(obs_tile, obs_site, batch_order, prior, wind, loc_bits.T)
    analysis = pl.pallas_call(
        filter_kernel,
        out_shape=jax.ShapeDtypeStruct((ROWS, 8, 128), BF16),
        in_specs=[spec(SM)] * 3 + [spec(VM)] * 2 + [spec(pl.ANY)],
        out_specs=spec(pl.ANY),
        scratch_shapes=[
            VM((128, 128), F32),
            VM((NOBS, 128), F32),
            VM((NOBS, 128), F32),
            VM((MEMBERS * 8, 128), F32),
            VM((PLANES, 2 * MEMBERS, CELLS), BF16),
            VM((ROWS, 8, 128), BF16),
            dma,
            dma((PLANES,)),
        ],
        name="filter",
    )(batch_order, obs_value, obs_var, masks, observed, forecast)
    return analysis.reshape(prior_state.shape)


def solution(mesh):
    placed = (
        P(None, None, None, "lat", "lon"),
        P(None, None, "lat", "lon"),
        P(),
        P(),
        P(),
        P(),
        P(),
        P(),
    )
    return jax.shard_map(
        per_device,
        mesh=mesh,
        in_specs=placed,
        out_specs=P(None, None, None, "lat", "lon"),
        check_vma=False,
    )
```
